256 devices in a mesh: orb: 64 (over y, z, core), rep: 4 (over x).
Axes of the slice: x: 4, y: 4, z: 8, core: 2. Of those that a mesh axis runs over, the one named last changes fastest.
Arguments:
- blocks: bfloat16 [128, 1024, 512], P('orb', 'rep'), may hold values from -1.078125 to 1.078125
- amplitudes: bfloat16 [512, 512, 512], P('orb', 'rep'), may hold values from -3 to 3
- pair_orbitals: int32 [512, 2], P('orb'), may hold values from 0 to 127, as said below
- coupling: int32 [512, 4], P('orb'), may hold values from 0 to 511, as said below
- fock_coupling: bfloat16 [512, 4], P('orb'), may hold values from -0.5 to 0.5
- virtual_energy: float32 [512], replicated, may hold values from 0.3 to 2
- occupied_energy: float32 [128], replicated, may hold values from -1.5 to -0.1
Outputs:
- updated_amplitudes: bfloat16 [512, 512, 512], P('orb', 'rep')
The draws below stay inside these ranges and needn't reach their ends.
Inputs may be any that keep to these rules, and one draw needn't show every extreme that they name: `pair_orbitals`: orbital o lives on owner o // 2 and pair p on owner p // 8. A pair's first orbital lies on the pair's owner; its second lies on the same owner or the next one. `coupling`: every coupled pair lies on the pair's owner or on an adjacent owner.
All inputs are finite; a program needn't handle non-finite values.
Results may differ from the reference program's by a relative error of at most 0.01.
Values may be sent and summed in bfloat16 or wider, within the bound.
No kernel may reach another device: no remote copies, remote signals or barrier semaphores. Data moves between devices by JAX's collectives and lax.ppermute only.
A program may use at most 64 MiB of HBM per device.

```python
import math
import jax
import jax.numpy as jnp
from jax import lax

NAUX = 1024
NV = 512
NCPL = 4
ORB_DEV = 2
PAIR_DEV = 8
AUXQ = 256
NOCC = 128
NPAIR = 512


def draw_pair_orbitals(key, part):
    owner_total = NPAIR // PAIR_DEV
    first_key = jax.random.fold_in(key, 11)
    second_key = jax.random.fold_in(key, 12)
    offset_key = jax.random.fold_in(key, 13)
    pair_owner = jnp.arange(NPAIR, dtype=jnp.int32) // PAIR_DEV
    first_orbital = pair_owner * ORB_DEV + jax.random.randint(first_key, (NPAIR,), 0, ORB_DEV, dtype=jnp.int32)
    next_owner = jnp.minimum(pair_owner + jax.random.randint(offset_key, (NPAIR,), 0, 2, dtype=jnp.int32), owner_total - 1)
    second_orbital = next_owner * ORB_DEV + jax.random.randint(second_key, (NPAIR,), 0, ORB_DEV, dtype=jnp.int32)
    return jnp.stack([first_orbital, second_orbital], axis=1).astype(jnp.int32)


def draw_coupling(key, part):
    owner_total = NPAIR // PAIR_DEV
    offset_key = jax.random.fold_in(key, 21)
    slot_key = jax.random.fold_in(key, 22)
    pair_owner = (jnp.arange(NPAIR, dtype=jnp.int32) // PAIR_DEV)[:, None]
    offsets = jax.random.randint(offset_key, (NPAIR, NCPL), -1, 2, dtype=jnp.int32)
    target_owner = jnp.clip(pair_owner + offsets, 0, owner_total - 1)
    slots = jax.random.randint(slot_key, (NPAIR, NCPL), 0, PAIR_DEV, dtype=jnp.int32)
    return (target_owner * PAIR_DEV + slots).astype(jnp.int32)


def shard_levels(rng, extent, cuts, low, top_value):
    factor_of = 1.0
    for dim, parts in cuts:
        heights = jax.random.uniform(jax.random.fold_in(jax.random.fold_in(rng, 6), dim), (parts,), jnp.float32, low / len(cuts), top_value / len(cuts))
        factor_of = factor_of * jnp.repeat(jnp.exp(heights), extent[dim] // parts).reshape((-1,) + (1,) * (len(extent) - 1 - dim))
    return factor_of


def normal_values(rng, extent, scale, bound, cuts=(), kind=jnp.bfloat16):
    level = shard_levels(rng, extent, cuts, -0.22, 0.18) if cuts else 1.0
    values = jax.random.normal(rng, extent, jnp.float32) * scale * level
    return jnp.minimum(jnp.maximum(values, -bound), bound).astype(kind)


def setup_inputs(seed: int = 0) -> dict:
    arg_keys = jax.random.split(jax.random.key(seed), 8)
    return {
        "blocks": normal_values(arg_keys[0], (NOCC, NAUX, NV), 0.18, 1.078125, ((0, 64), (1, 4))),
        "amplitudes": normal_values(arg_keys[1], (NPAIR, NV, NV), 0.5, 3.0, ((0, 64), (1, 4))),
        "pair_orbitals": draw_pair_orbitals(jax.random.fold_in(arg_keys[7], 71), 0),
        "coupling": draw_coupling(jax.random.fold_in(arg_keys[7], 71), 0),
        "fock_coupling": jnp.clip(jax.random.uniform(arg_keys[4], (NPAIR, NCPL), jnp.float32, -0.5, 0.5) * shard_levels(arg_keys[4], (NPAIR, NCPL), ((0, 64),), -0.4, 0.0), -0.5, 0.5).astype(jnp.bfloat16),
        "virtual_energy": jnp.clip(jnp.exp(jax.random.uniform(arg_keys[5], (NV,), jnp.float32, math.log(0.3), math.log(2.0))), 0.3, 2.0),
        "occupied_energy": jnp.clip(jax.random.uniform(arg_keys[6], (NOCC,), jnp.float32, -1.5, -0.1), -1.5, -0.1),
    }


damping = 0.7


def reference(blocks, amplitudes, pair_orbitals, coupling, fock_coupling, virtual_energy, occupied_energy):
    def one_pair(pair_index):
        first_orbital = pair_orbitals[pair_index, 0]
        second_orbital = pair_orbitals[pair_index, 1]
        left_block = blocks[first_orbital].astype(jnp.float32).reshape(NAUX // AUXQ, AUXQ, NV)
        right_block = blocks[second_orbital].astype(jnp.float32).reshape(NAUX // AUXQ, AUXQ, NV)
        partial_value = jnp.einsum("gqa,gqb->gab", left_block, right_block, precision=lax.Precision.HIGHEST)
        rounded = lax.optimization_barrier(partial_value.astype(jnp.bfloat16))
        integrals = jnp.sum(rounded.astype(jnp.float32), axis=0)
        picked = amplitudes[coupling[pair_index]].astype(jnp.float32)
        weights = fock_coupling[pair_index].astype(jnp.float32)
        coupled = jnp.einsum("c,cab->ab", weights, picked, precision=lax.Precision.HIGHEST)
        pair_shift = occupied_energy[first_orbital] + occupied_energy[second_orbital]
        denominator = virtual_energy[:, None] + virtual_energy[None, :] - pair_shift
        previous = amplitudes[pair_index].astype(jnp.float32)
        updated = (1.0 - damping) * previous - damping * (integrals - coupled) / denominator
        return updated.astype(jnp.bfloat16)

    return lax.map(one_pair, jnp.arange(NPAIR, dtype=jnp.int32))
```

```python
import functools
import jax
import jax.numpy as jnp
from jax import lax
from jax.experimental import pallas as pl
from jax.experimental.pallas import tpu as pltpu
from jax.sharding import PartitionSpec as P

damping = 0.7


SMEM = pl.BlockSpec(memory_space=pltpu.SMEM)
VMEM = pl.BlockSpec(memory_space=pltpu.VMEM)
ANY = pl.BlockSpec(memory_space=pl.ANY)


def shifted_orb(x, distance):
    n = lax.axis_size("orb")
    route = [(i - distance, i) for i in range(n) if 0 <= i - distance < n]
    return lax.ppermute(x, "orb", route)


def shifted_rep(x, distance):
    n = lax.axis_size("rep")
    return lax.ppermute(x, "rep", [(i, (i + distance) % n) for i in range(n)])


def shifted_rep_odd(x, distance):
    n, m = lax.axis_size("orb"), lax.axis_size("rep")
    route = [(o * m + i, o * m + (i + distance) % m) for o in range(1, n, 2) for i in range(m)]
    return lax.ppermute(x, ("orb", "rep"), route)


def odd_to_even(x):
    n = lax.axis_size("orb")
    return lax.ppermute(x, "orb", [(o, o - 1) for o in range(1, n, 2)])


def couple_kernel(ids, orbs, cpl, fock, occ, row_e, col_e, prev, own, nxt, pre, wgt, amps, sems):
    pair_count = own.shape[0]
    copies = [
        pltpu.make_async_copy(src, amps.at[pl.ds(k * pair_count, pair_count)], sems.at[k])
        for k, src in enumerate((prev, own, nxt))
    ]
    for c in copies:
        c.start()
    for c in copies:
        c.wait()
    base = (ids[0] - 1) * pair_count
    rows = pre.shape[1]
    step = 32

    def pair(p, carry):
        shift = occ[orbs[p, 0]] + occ[orbs[p, 1]]
        slots = [cpl[p, c] - base for c in range(cpl.shape[1])]
        weights = [fock[p, c] for c in range(cpl.shape[1])]

        for r in range(0, rows, step):
            part = pl.ds(r, step)
            w = damping / (row_e[part, :] + (col_e[...] - shift))
            total = None
            for s, f in zip(slots, weights):
                term = f * amps[s, part, :].astype(jnp.float32)
                total = term if total is None else total + term
            mine = amps[p + pair_count, part, :].astype(jnp.float32)
            pre[p, part, :] = (1.0 - damping) * mine + w * total
            wgt[p, part, :] = w
        return carry

    lax.fori_loop(0, pair_count, pair, 0)


def coupled_terms(ids, orbs, cpl, fock, occ, row_e, col_e, prev, own, nxt):
    shape = jax.ShapeDtypeStruct(own.shape, jnp.float32)
    return pl.pallas_call(
        couple_kernel,
        out_shape=(shape, shape),
        in_specs=[SMEM] * 5 + [VMEM] * 2 + [ANY] * 3,
        out_specs=(VMEM, VMEM),
        scratch_shapes=[
            pltpu.VMEM((3 * own.shape[0],) + own.shape[1:], own.dtype),
            pltpu.SemaphoreType.DMA((3,)),
        ],
        compiler_params=pltpu.CompilerParams(vmem_limit_bytes=16 * 2**20),
        cost_estimate=pl.CostEstimate(flops=10**7, bytes_accessed=7 * 2**20, transcendentals=0),
        name="coupled_terms",
    )(ids, orbs, cpl, fock, occ, row_e, col_e, prev, own, nxt)


def dot_t(a, b):
    return lax.dot_general(a, b, (((0,), (0,)), ((), ())), preferred_element_type=jnp.float32)


def rows_of(ref, i, start, width):
    return ref[i, :, pl.ds(start, width)]


def left_of(ref, start, width):
    return jnp.concatenate([rows_of(ref, i, start, width) for i in range(ref.shape[0])], axis=1)


def own_kernel(ids, b0, b1, b2, out):
    orbitals, _, width = b0.shape
    rows = out.shape[2]
    start = pl.multiple_of(ids[1] * rows, rows)
    left = jnp.concatenate([left_of(b, start, rows) for b in (b0, b1, b2)], axis=0)
    for j in range(orbitals):
        right = jnp.concatenate([b[j] for b in (b0, b1, b2)], axis=0)
        both = dot_t(left, right)
        for i in range(orbitals):
            out[i, j] = both[i * rows:(i + 1) * rows]


def own_part(ids, b0, b1, b2):
    orbitals, _, width = b0.shape
    rows = width // lax.axis_size("rep")
    return pl.pallas_call(
        own_kernel,
        out_shape=jax.ShapeDtypeStruct((orbitals, orbitals, rows, width), jnp.float32),
        in_specs=[SMEM] + [VMEM] * 3,
        out_specs=VMEM,
        compiler_params=pltpu.CompilerParams(vmem_limit_bytes=16 * 2**20),
        cost_estimate=pl.CostEstimate(flops=4 * 10**8, bytes_accessed=3 * 2**20, transcendentals=0),
        name="own_part",
    )(ids, b0, b1, b2)


def next_kernel(ids, b0, b1, b2, n0, n1x, n1c, n2x, n2c, out):
    orbitals, _, width = b0.shape
    rows = out.shape[2]
    start = pl.multiple_of(ids[1] * rows, rows)
    odd = lax.rem(ids[0], 2) == 1
    left = jnp.concatenate([left_of(b, start, rows) for b in (b0, b1, b2)], axis=0)
    for j in range(orbitals):
        right = jnp.concatenate(
            [n0[j], jnp.where(odd, n1x[j], n1c[j]), jnp.where(odd, n2x[j], n2c[j])], axis=0
        )
        both = dot_t(left, right)
        for i in range(orbitals):
            out[i, j] = both[i * rows:(i + 1) * rows]


def next_part(ids, b0, b1, b2, *right):
    orbitals, _, width = b0.shape
    rows = width // lax.axis_size("rep")
    return pl.pallas_call(
        next_kernel,
        out_shape=jax.ShapeDtypeStruct((orbitals, orbitals, rows, width), jnp.float32),
        in_specs=[SMEM] + [VMEM] * 8,
        out_specs=VMEM,
        compiler_params=pltpu.CompilerParams(vmem_limit_bytes=16 * 2**20),
        cost_estimate=pl.CostEstimate(flops=4 * 10**8, bytes_accessed=5 * 2**20, transcendentals=0),
        name="next_part",
    )(ids, b0, b1, b2, *right)


def update_kernel(ids, orbs, own_acc, next_acc, pre, wgt, b3, n3, out, acc):
    orbitals = own_acc.shape[0]
    rows = out.shape[1]
    pair_count = out.shape[0]
    start = pl.multiple_of(ids[1] * rows, rows)
    left = jnp.concatenate([b[0, :, pl.ds(start, rows)] for b in b3], axis=1)
    for j in range(orbitals):
        both = dot_t(left, b3[j][0])
        after = dot_t(left, n3[j][0])
        for i in range(orbitals):
            part = slice(i * rows, (i + 1) * rows)
            acc[i * 2 * orbitals + j] = own_acc[i, j] + both[part]
            acc[i * 2 * orbitals + orbitals + j] = next_acc[i, j] + after[part]
    base = ids[0] * orbitals

    def pair(p, carry):
        slot = (orbs[p, 0] - base) * 2 * orbitals + (orbs[p, 1] - base)
        out[p] = (pre[p] - wgt[p] * acc[slot]).astype(out.dtype)
        return carry

    lax.fori_loop(0, pair_count, pair, 0)


def updated(ids, orbs, own_acc, next_acc, pre, wgt, b3, n3):
    def body(ids, orbs, own_acc, next_acc, pre, wgt, b30, b31, n30, n31, out, acc):
        update_kernel(ids, orbs, own_acc, next_acc, pre, wgt, (b30, b31), (n30, n31), out, acc)

    orbitals, _, rows, width = own_acc.shape
    return pl.pallas_call(
        body,
        out_shape=jax.ShapeDtypeStruct(pre.shape, jnp.bfloat16),
        in_specs=[SMEM] * 2 + [VMEM] * 8,
        out_specs=VMEM,
        scratch_shapes=[pltpu.VMEM((2 * orbitals * orbitals, rows, width), jnp.float32)],
        compiler_params=pltpu.CompilerParams(vmem_limit_bytes=20 * 2**20),
        cost_estimate=pl.CostEstimate(flops=3 * 10**8, bytes_accessed=8 * 2**20, transcendentals=0),
        name="updated",
    )(ids, orbs, own_acc, next_acc, pre, wgt, *b3, *n3)


def per_device(
    blocks, amplitudes, pair_orbitals, coupling, fock_coupling, virtual_energy, occupied_energy
):
    row_count = amplitudes.shape[1]
    owner = lax.axis_index("orb").astype(jnp.int32)
    replica = lax.axis_index("rep").astype(jnp.int32)
    ids = jnp.stack([owner, replica])
    b0 = blocks
    n0 = shifted_orb(b0, -1)
    b1 = shifted_rep(b0, 1)
    b2 = shifted_rep(b0, -1)
    amps_prev = shifted_orb(amplitudes, 1)
    amps_next = shifted_orb(amplitudes, -1)
    b3 = (shifted_rep(b1[0:1], 1), shifted_rep(b2[1:2], -1))
    n1x = shifted_rep_odd(n0, 1)
    n2x = shifted_rep_odd(n0, -1)
    n1c = odd_to_even(b1)
    n2c = odd_to_even(b2)
    n3 = tuple(shifted_orb(b, -1) for b in b3)
    row_e = lax.dynamic_slice_in_dim(virtual_energy, replica * row_count, row_count)[:, None]
    pre, wgt = coupled_terms(
        ids, pair_orbitals, coupling, fock_coupling.astype(jnp.float32), occupied_energy,
        row_e, virtual_energy[None, :], amps_prev, amplitudes, amps_next,
    )
    own_acc = own_part(ids, b0, b1, b2)
    next_acc = next_part(ids, b0, b1, b2, n0, n1x, n1c, n2x, n2c)
    return updated(ids, pair_orbitals, own_acc, next_acc, pre, wgt, b3, n3)


def solution(mesh):
    placed = (
        P("orb", "rep", None),
        P("orb", "rep", None),
        P("orb", None),
        P("orb", None),
        P("orb", None),
        P(),
        P(),
    )
    return jax.shard_map(
        per_device, mesh=mesh, in_specs=placed, out_specs=P("orb", "rep", None), check_vma=False
    )
```

```python
import jax
import jax.numpy as jnp
from jax import lax
from jax.experimental import pallas as pl
from jax.experimental.pallas import tpu as pltpu
from jax.sharding import PartitionSpec as P

damping = 0.7


SMEM = pl.BlockSpec(memory_space=pltpu.SMEM)
VMEM = pl.BlockSpec(memory_space=pltpu.VMEM)
ANY = pl.BlockSpec(memory_space=pl.ANY)


def along_orb(x, distance):
    n = lax.axis_size("orb")
    return lax.ppermute(x, "orb", [(i - distance, i) for i in range(n) if 0 <= i - distance < n])


def along_rep(x, distance):
    n = lax.axis_size("rep")
    return lax.ppermute(x, "rep", [(i, (i + distance) % n) for i in range(n)])


def along_rep_odd(x, distance):
    n, m = lax.axis_size("orb"), lax.axis_size("rep")
    route = [(o * m + i, o * m + (i + distance * (o % 2)) % m) for o in range(n) for i in range(m)]
    return lax.ppermute(x, ("orb", "rep"), route)


def odd_to_even(x):
    n = lax.axis_size("orb")
    return lax.ppermute(x, "orb", [(o, o - 1) for o in range(1, n, 2)])


def call(body, out_shape, in_specs, scratch=(), limit=16, cost=10**8):
    return pl.pallas_call(
        body,
        out_shape=out_shape,
        in_specs=in_specs,
        out_specs=jax.tree.map(lambda _: VMEM, out_shape),
        scratch_shapes=list(scratch),
        compiler_params=pltpu.CompilerParams(vmem_limit_bytes=limit * 2**20),
        cost_estimate=pl.CostEstimate(flops=cost, bytes_accessed=4 * 2**20, transcendentals=0),
    )


def couple_kernel(ids, orbs, cpl, fock, occ, row_e, col_e, prev, own, nxt, pre, wgt, amps, sems):
    pair_count, rows = own.shape[:2]
    copies = [
        pltpu.make_async_copy(src, amps.at[pl.ds(k * pair_count, pair_count)], sems.at[k])
        for k, src in enumerate((prev, own, nxt))
    ]
    for c in copies:
        c.start()
    for c in copies:
        c.wait()
    base = (ids[0] - 1) * pair_count
    step = 32

    def pair(p, carry):
        shift = occ[orbs[0, p]] + occ[orbs[1, p]]
        slots = [cpl[c, p] - base for c in range(cpl.shape[0])]
        weights = [fock[c, p] for c in range(cpl.shape[0])]
        for r in range(0, rows, step):
            part = pl.ds(r, step)
            w = damping / (row_e[part, :] + (col_e[...] - shift))
            total = None
            for s, f in zip(slots, weights):
                term = f * amps[s, part, :].astype(jnp.float32)
                total = term if total is None else total + term
            mine = amps[p + pair_count, part, :].astype(jnp.float32)
            pre[p, part, :] = (1.0 - damping) * mine + w * total
            wgt[p, part, :] = w
        return carry

    lax.fori_loop(0, pair_count, pair, 0)


def coupled_terms(*args):
    own = args[-2]
    shape = jax.ShapeDtypeStruct(own.shape, jnp.float32)
    scratch = (
        pltpu.VMEM((3 * own.shape[0],) + own.shape[1:], own.dtype),
        pltpu.SemaphoreType.DMA((3,)),
    )
    specs = [SMEM] * 5 + [VMEM] * 2 + [ANY] * 3
    return call(couple_kernel, (shape, shape), specs, scratch)(*args)


def dot_t(a, b):
    return lax.dot_general(a, b, (((0,), (0,)), ((), ())), preferred_element_type=jnp.float32)


def left_of(ids, blocks, rows):
    start = pl.multiple_of(ids[1] * rows, rows)
    return jnp.concatenate(
        [
            jnp.concatenate([b[i, :, pl.ds(start, rows)] for i in range(b.shape[0])], axis=1)
            for b in blocks
        ],
        axis=0,
    )


def products(ids, left, right, out):
    orbitals, _, rows, _ = out.shape
    lhs = left_of(ids, left, rows)
    for j in range(orbitals):
        both = dot_t(lhs, jnp.concatenate([r(j) for r in right], axis=0))
        for i in range(orbitals):
            out[i, j] = both[i * rows:(i + 1) * rows]


def acc_shape(block):
    orbitals, _, width = block.shape
    return jax.ShapeDtypeStruct(
        (orbitals, orbitals, width // lax.axis_size("rep"), width), jnp.float32
    )


def whole(ref):
    return lambda j: ref[j]


def either(ids, odd_ref, even_ref):
    odd = lax.rem(ids[0], 2) == 1
    return lambda j: jnp.where(odd, odd_ref[j], even_ref[j])


def own_part(ids, b0, b1, b2):
    def body(ids, b0, b1, b2, out):
        products(ids, (b0, b1, b2), [whole(b) for b in (b0, b1, b2)], out)

    return call(body, acc_shape(b0), [SMEM] + [VMEM] * 3)(ids, b0, b1, b2)


def next_part(ids, b0, b1, b2, n0, n1, n2x, n2c):
    def body(ids, b0, b1, b2, n0, n1, n2x, n2c, out):
        products(ids, (b0, b1, b2), [whole(n0), whole(n1), either(ids, n2x, n2c)], out)

    return call(body, acc_shape(b0), [SMEM] + [VMEM] * 7)(ids, b0, b1, b2, n0, n1, n2x, n2c)


def pair_slot(ids, orbs, p, orbitals):
    base = ids[0] * orbitals
    return orbs[0, p] - base, orbs[1, p] - base


def partial_update(ids, orbs, own_acc, next_acc, pre, wgt, b3):
    def body(ids, orbs, own_acc, next_acc, pre, wgt, b3, out, acc):
        orbitals, _, rows, _ = own_acc.shape
        lhs = left_of(ids, (b3,), rows)
        for j in range(orbitals):
            both = dot_t(lhs, b3[j])
            for i in range(orbitals):
                acc[i, j] = own_acc[i, j] + both[i * rows:(i + 1) * rows]
                acc[i, orbitals + j] = next_acc[i, j]

        def pair(p, carry):
            i, j = pair_slot(ids, orbs, p, orbitals)
            out[p] = pre[p] - wgt[p] * acc[i, j]
            return carry

        lax.fori_loop(0, out.shape[0], pair, 0)

    o, _, r, w = own_acc.shape
    return call(
        body, jax.ShapeDtypeStruct(pre.shape, jnp.float32),
        [SMEM] * 2 + [VMEM] * 5, [pltpu.VMEM((o, 2 * o, r, w), jnp.float32)],
    )(ids, orbs, own_acc, next_acc, pre, wgt, b3)


def last_update(ids, orbs, part, wgt, b3, n3x, n3c):
    def body(ids, orbs, part, wgt, b3, n3x, n3c, out, acc):
        orbitals, _, _, _ = acc.shape
        products(ids, (b3,), [either(ids, n3x, n3c)], acc)

        def pair(p, carry):
            i, j = pair_slot(ids, orbs, p, orbitals)
            ahead = j >= orbitals

            @pl.when(ahead)
            def _():
                out[p] = (part[p] - wgt[p] * acc[i, j - orbitals]).astype(out.dtype)

            @pl.when(jnp.logical_not(ahead))
            def _():
                out[p] = part[p].astype(out.dtype)

            return carry

        lax.fori_loop(0, out.shape[0], pair, 0)

    acc = acc_shape(b3)
    return call(
        body, jax.ShapeDtypeStruct(part.shape, jnp.bfloat16),
        [SMEM] * 2 + [VMEM] * 5, [pltpu.VMEM(acc.shape, acc.dtype)],
    )(ids, orbs, part, wgt, b3, n3x, n3c)


def device_step(
    blocks, amplitudes, pair_orbitals, coupling, fock_coupling, virtual_energy, occupied_energy
):
    row_count = amplitudes.shape[1]
    owner = lax.axis_index("orb").astype(jnp.int32)
    replica = lax.axis_index("rep").astype(jnp.int32)
    ids = jnp.stack([owner, replica])
    orbs = pair_orbitals.T
    b0 = blocks
    n0 = along_orb(b0, -1)
    b1 = along_rep(b0, 1)
    b2 = along_rep(b0, -1)
    amps_next = along_orb(amplitudes, -1)
    amps_prev = along_orb(amplitudes, 1)
    n2x = along_rep_odd(n0, -1)
    b3 = along_rep(b1, 1)
    n1 = along_orb(b1, -1)
    n2c = odd_to_even(b2)
    n3x = along_rep_odd(n2x, -1)
    n3c = odd_to_even(b3)
    row_e = lax.dynamic_slice_in_dim(virtual_energy, replica * row_count, row_count)[:, None]
    pre, wgt = coupled_terms(
        ids, orbs, coupling.T, fock_coupling.T.astype(jnp.float32), occupied_energy,
        row_e, virtual_energy[None, :], amps_prev, amplitudes, amps_next,
    )
    own_acc = own_part(ids, b0, b1, b2)
    next_acc = next_part(ids, b0, b1, b2, n0, n1, n2x, n2c)
    part = partial_update(ids, orbs, own_acc, next_acc, pre, wgt, b3)
    return last_update(ids, orbs, part, wgt, b3, n3x, n3c)


def solution(mesh):
    placed = (
        P("orb", "rep", None),
        P("orb", "rep", None),
        P("orb", None),
        P("orb", None),
        P("orb", None),
        P(),
        P(),
    )
    return jax.shard_map(
        device_step, mesh=mesh, in_specs=placed, out_specs=P("orb", "rep", None), check_vma=False
    )
```

```python
import jax
import jax.numpy as jnp
from jax import lax
from jax.experimental import pallas as pl
from jax.experimental.pallas import tpu as pltpu
from jax.sharding import PartitionSpec as P

damping = 0.7


SMEM = pl.BlockSpec(memory_space=pltpu.SMEM)
VMEM = pl.BlockSpec(memory_space=pltpu.VMEM)
ANY = pl.BlockSpec(memory_space=pl.ANY)


def along_orb(x, distance):
    n = lax.axis_size("orb")
    return lax.ppermute(x, "orb", [(i - distance, i) for i in range(n) if 0 <= i - distance < n])


def along_rep(x, distance):
    n = lax.axis_size("rep")
    return lax.ppermute(x, "rep", [(i, (i + distance) % n) for i in range(n)])


def along_rep_odd(x, distance):
    n, m = lax.axis_size("orb"), lax.axis_size("rep")
    route = [(o * m + i, o * m + (i + distance * (o % 2)) % m) for o in range(n) for i in range(m)]
    return lax.ppermute(x, ("orb", "rep"), route)


def odd_to_even(x):
    n = lax.axis_size("orb")
    return lax.ppermute(x, "orb", [(o, o - 1) for o in range(1, n, 2)])


def call(body, out_shape, in_specs, scratch=(), out_specs=None, limit=16):
    return pl.pallas_call(
        body,
        out_shape=out_shape,
        in_specs=in_specs,
        out_specs=out_specs or jax.tree.map(lambda _: VMEM, out_shape),
        scratch_shapes=list(scratch),
        compiler_params=pltpu.CompilerParams(vmem_limit_bytes=limit * 2**20),
        cost_estimate=pl.CostEstimate(flops=10**8, bytes_accessed=4 * 2**20, transcendentals=0),
    )


def couple_kernel(ids, orbs, cpl, fock, occ, mine, energy, prev, own, nxt, pre, wgt, amps, sems):
    pair_count, rows = own.shape[:2]
    copies = [
        pltpu.make_async_copy(src, amps.at[pl.ds(k * pair_count, pair_count)], sems.at[k])
        for k, src in enumerate((prev, own, nxt))
    ]
    for c in copies:
        c.start()
    tile = jnp.broadcast_to(mine[...], (rows, rows))

    def denominators(p, carry):
        shift = occ[orbs[0, p]] + occ[orbs[1, p]]
        for c in range(0, energy.shape[1], rows):
            part = slice(c, c + rows)
            wgt[p, :, part] = damping / (tile + (energy[:, part] - shift))
        return carry

    lax.fori_loop(0, pair_count, denominators, 0)
    for c in copies:
        c.wait()
    base = (ids[0] - 1) * pair_count
    step = 32

    def pair(p, carry):
        slots = [cpl[c, p] - base for c in range(cpl.shape[0])]
        scales = [fock[c, p] for c in range(cpl.shape[0])]
        for r in range(0, rows, step):
            part = pl.ds(r, step)
            total = None
            for s, f in zip(slots, scales):
                term = f * amps[s, part, :].astype(jnp.float32)
                total = term if total is None else total + term
            mine = amps[p + pair_count, part, :].astype(jnp.float32)
            pre[p, part, :] = (1.0 - damping) * mine + wgt[p, part, :] * total
        return carry

    lax.fori_loop(0, pair_count, pair, 0)


def coupled_terms(*args):
    own = args[-2]
    shape = jax.ShapeDtypeStruct(own.shape, jnp.float32)
    scratch = (
        pltpu.VMEM((3 * own.shape[0],) + own.shape[1:], own.dtype),
        pltpu.SemaphoreType.DMA((3,)),
    )
    specs = [SMEM] * 5 + [VMEM] * 2 + [ANY] * 3
    return call(couple_kernel, (shape, shape), specs, scratch)(*args)


def dot_t(a, b):
    return lax.dot_general(a, b, (((0,), (0,)), ((), ())), preferred_element_type=jnp.float32)


def left_of(ids, blocks, rows):
    start = pl.multiple_of(ids[1] * rows, rows)
    return jnp.concatenate(
        [
            jnp.concatenate([b[i, :, pl.ds(start, rows)] for i in range(b.shape[0])], axis=1)
            for b in blocks
        ],
        axis=0,
    )


def products(ids, left, right, out):
    orbitals, _, rows, _ = out.shape
    lhs = left_of(ids, left, rows)
    for j in range(orbitals):
        both = dot_t(lhs, jnp.concatenate([r(j) for r in right], axis=0))
        for i in range(orbitals):
            out[i, j] = both[i * rows:(i + 1) * rows]


def acc_shape(block):
    orbitals, _, width = block.shape
    return jax.ShapeDtypeStruct(
        (orbitals, orbitals, width // lax.axis_size("rep"), width), jnp.float32
    )


def whole(ref):
    return lambda j: ref[j]


def either(ids, odd_ref, even_ref):
    odd = lax.rem(ids[0], 2) == 1
    return lambda j: jnp.where(odd, odd_ref[j], even_ref[j])


def own_part(ids, b0, b1, b2):
    def body(ids, b0, b1, b2, out):
        products(ids, (b0, b1, b2), [whole(b) for b in (b0, b1, b2)], out)

    return call(body, acc_shape(b0), [SMEM] + [VMEM] * 3)(ids, b0, b1, b2)


def next_part(ids, b0, b1, b2, n0, n1, n2x, n2c):
    def body(ids, b0, b1, b2, n0, n1, n2x, n2c, out):
        products(ids, (b0, b1, b2), [whole(n0), whole(n1), either(ids, n2x, n2c)], out)

    return call(body, acc_shape(b0), [SMEM] + [VMEM] * 7)(ids, b0, b1, b2, n0, n1, n2x, n2c)


def pair_slot(ids, orbs, p, orbitals):
    base = ids[0] * orbitals
    return orbs[0, p] - base, orbs[1, p] - base


def partial_update(ids, orbs, own_acc, next_acc, pre, wgt, b3):
    def body(ids, orbs, own_acc, next_acc, pre, wgt, b3, out, acc):
        orbitals, _, rows, _ = own_acc.shape
        lhs = left_of(ids, (b3,), rows)
        for j in range(orbitals):
            both = dot_t(lhs, b3[j])
            for i in range(orbitals):
                acc[i, j] = own_acc[i, j] + both[i * rows:(i + 1) * rows]

        def pair(p, carry):
            i, j = pair_slot(ids, orbs, p, orbitals)

            @pl.when(j < orbitals)
            def _():
                out[p] = pre[p] - wgt[p] * acc[i, j]

            @pl.when(j >= orbitals)
            def _():
                out[p] = pre[p] - wgt[p] * next_acc[i, j - orbitals]

            return carry

        lax.fori_loop(0, out.shape[0], pair, 0)

    return call(
        body, jax.ShapeDtypeStruct(pre.shape, jnp.float32),
        [SMEM] * 2 + [VMEM] * 5, [pltpu.VMEM(own_acc.shape, own_acc.dtype)],
    )(ids, orbs, own_acc, next_acc, pre, wgt, b3)


def last_update(ids, orbs, part, wgt, left, n3x, n3c):
    def body(ids, orbs, part, wgt, left, n3x, n3c, out, acc, done, sem):
        orbitals = acc.shape[0]
        products(ids, (left,), [either(ids, n3x, n3c)], acc)

        def pair(p, carry):
            i, j = pair_slot(ids, orbs, p, orbitals)

            @pl.when(j >= orbitals)
            def _():
                done[p] = (part[p] - wgt[p] * acc[i, j - orbitals]).astype(done.dtype)

            @pl.when(j < orbitals)
            def _():
                done[p] = part[p].astype(done.dtype)

            pltpu.make_async_copy(done.at[p], out.at[p], sem.at[p]).start()
            return carry

        def wait(p, carry):
            pltpu.make_async_copy(done.at[p], out.at[p], sem.at[p]).wait()
            return carry

        lax.fori_loop(0, done.shape[0], pair, 0)
        lax.fori_loop(0, done.shape[0], wait, 0)

    acc = acc_shape(n3x)
    scratch = [
        pltpu.VMEM(acc.shape, acc.dtype),
        pltpu.VMEM(part.shape, jnp.bfloat16),
        pltpu.SemaphoreType.DMA((part.shape[0],)),
    ]
    return call(
        body, jax.ShapeDtypeStruct(part.shape, jnp.bfloat16),
        [SMEM] * 2 + [VMEM] * 5, scratch, out_specs=ANY,
    )(ids, orbs, part, wgt, left, n3x, n3c)


def device_step(
    blocks, amplitudes, pair_orbitals, coupling, fock_coupling, virtual_energy, occupied_energy
):
    owner = lax.axis_index("orb").astype(jnp.int32)
    replica = lax.axis_index("rep").astype(jnp.int32)
    ids = jnp.stack([owner, replica])
    orbs = pair_orbitals.T
    b0 = blocks
    n0 = along_orb(b0, -1)
    b1 = along_rep(b0, 1)
    b2 = along_rep(b0, -1)
    amps_next = along_orb(amplitudes, -1)
    amps_prev = along_orb(amplitudes, 1)
    n2x = along_rep_odd(n0, -1)
    b3 = along_rep(b1, 1)
    n1 = along_orb(b1, -1)
    n2c = odd_to_even(b2)
    n3x = along_rep_odd(n2x, -1)
    n3c = odd_to_even(b3)
    rows = amplitudes.shape[1]
    row_e = lax.dynamic_slice_in_dim(virtual_energy, replica * rows, rows)[:, None]
    fock = fock_coupling.T.astype(jnp.float32)
    pre, wgt = coupled_terms(
        ids, orbs, coupling.T, fock, occupied_energy, row_e, virtual_energy[None, :],
        amps_prev, amplitudes, amps_next,
    )
    own_acc = own_part(ids, b0, b1, b2)
    next_acc = next_part(ids, b0, b1, b2, n0, n1, n2x, n2c)
    part = partial_update(ids, orbs, own_acc, next_acc, pre, wgt, b3)
    return last_update(ids, orbs, part, wgt, b3, n3x, n3c)


def solution(mesh):
    placed = (
        P("orb", "rep", None),
        P("orb", "rep", None),
        P("orb", None),
        P("orb", None),
        P("orb", None),
        P(),
        P(),
    )
    return jax.shard_map(
        device_step, mesh=mesh, in_specs=placed, out_specs=P("orb", "rep", None), check_vma=False
    )
```

```python
import jax
import jax.numpy as jnp
from jax import lax
from jax.experimental import pallas as pl
from jax.experimental.pallas import tpu as pltpu
from jax.sharding import PartitionSpec as P

damping = 0.7


SMEM = pl.BlockSpec(memory_space=pltpu.SMEM)
VMEM = pl.BlockSpec(memory_space=pltpu.VMEM)
ANY = pl.BlockSpec(memory_space=pl.ANY)


def along_orb(x, distance):
    n = lax.axis_size("orb")
    return lax.ppermute(x, "orb", [(i - distance, i) for i in range(n) if 0 <= i - distance < n])


def along_rep(x, distance):
    n = lax.axis_size("rep")
    return lax.ppermute(x, "rep", [(i, (i + distance) % n) for i in range(n)])


def along_rep_odd(x, distance):
    n, m = lax.axis_size("orb"), lax.axis_size("rep")
    route = [(o * m + i, o * m + (i + distance * (o % 2)) % m) for o in range(n) for i in range(m)]
    return lax.ppermute(x, ("orb", "rep"), route)


def diagonal(x, distance):
    n, m = lax.axis_size("orb"), lax.axis_size("rep")
    route = [(o * m + i, (o - 1) * m + i) for o in range(1, n, 2) for i in range(m)]
    route += [
        (o * m + i, (o - 1) * m + (i + distance) % m) for o in range(2, n, 2) for i in range(m)
    ]
    return lax.ppermute(x, ("orb", "rep"), route)


def odd_to_even(x):
    n = lax.axis_size("orb")
    return lax.ppermute(x, "orb", [(o, o - 1) for o in range(1, n, 2)])


def swapped(x):
    n = lax.axis_size("orb")
    return lax.ppermute(x, "orb", [(o, o ^ 1) for o in range(n)])


def call(body, out_shape, in_specs, scratch=(), out_specs=None, limit=16):
    return pl.pallas_call(
        body,
        out_shape=out_shape,
        in_specs=in_specs,
        out_specs=out_specs or jax.tree.map(lambda _: VMEM, out_shape),
        scratch_shapes=list(scratch),
        compiler_params=pltpu.CompilerParams(vmem_limit_bytes=limit * 2**20),
        cost_estimate=pl.CostEstimate(flops=10**8, bytes_accessed=4 * 2**20, transcendentals=0),
    )


def couple_kernel(
    orb, rep, ints, fock, occ, energies, prev, own, nxt, pre, wgt, amps, sems
):
    first = energies.shape[1] - own.shape[2]
    pair_count, rows = own.shape[:2]
    copies = [
        pltpu.make_async_copy(src, amps.at[pl.ds(k * pair_count, pair_count)], sems.at[k])
        for k, src in enumerate((prev, own, nxt))
    ]
    for c in copies:
        c.start()
    mine = energies[:, pl.ds(pl.multiple_of(first + rep[0] * rows, rows), rows)]
    tile = jnp.transpose(jnp.broadcast_to(mine, (rows, rows)))

    def denominators(p, carry):
        shift = occ[0, ints[0, p]] + occ[0, ints[1, p]]
        for c in range(0, own.shape[2], rows):
            row = energies[:, first + c:first + c + rows]
            wgt[p, :, c:c + rows] = damping / (tile + (row - shift))
        return carry

    lax.fori_loop(0, pair_count, denominators, 0)
    for c in copies:
        c.wait()
    base = (orb[0] - 1) * pair_count
    step = 32

    def pair(p, carry):
        slots = [ints[2 + c, p] - base for c in range(fock.shape[0])]
        scales = [fock[c, p] for c in range(fock.shape[0])]
        for r in range(0, rows, step):
            part = pl.ds(r, step)
            total = None
            for s, f in zip(slots, scales):
                term = f * amps[s, part, :].astype(jnp.float32)
                total = term if total is None else total + term
            mine = amps[p + pair_count, part, :].astype(jnp.float32)
            pre[p, part, :] = (1.0 - damping) * mine + wgt[p, part, :] * total
        return carry

    lax.fori_loop(0, pair_count, pair, 0)


def coupled_terms(*args):
    own = args[-2]
    shape = jax.ShapeDtypeStruct(own.shape, jnp.float32)
    scratch = (
        pltpu.VMEM((3 * own.shape[0],) + own.shape[1:], own.dtype),
        pltpu.SemaphoreType.DMA((3,)),
    )
    specs = [SMEM] * 5 + [VMEM] + [ANY] * 3
    return call(couple_kernel, (shape, shape), specs, scratch)(*args)


def dot_t(a, b):
    return lax.dot_general(a, b, (((0,), (0,)), ((), ())), preferred_element_type=jnp.float32)


def left_of(rep, blocks, rows):
    start = pl.multiple_of(rep[0] * rows, rows)
    return jnp.concatenate(
        [
            jnp.concatenate([b[i, :, pl.ds(start, rows)] for i in range(b.shape[0])], axis=1)
            for b in blocks
        ],
        axis=0,
    )


def products(rep, left, right, out):
    orbitals, _, rows, _ = out.shape
    lhs = left_of(rep, left, rows)
    for j in range(orbitals):
        both = dot_t(lhs, jnp.concatenate([r(j) for r in right], axis=0))
        for i in range(orbitals):
            out[i, j] = both[i * rows:(i + 1) * rows]


def acc_shape(block):
    orbitals, _, width = block.shape
    return jax.ShapeDtypeStruct(
        (orbitals, orbitals, width // lax.axis_size("rep"), width), jnp.float32
    )


def whole(ref):
    return lambda j: ref[j]


def either(orb, odd_ref, even_ref):
    odd = lax.rem(orb[0], 2) == 1
    return lambda j: jnp.where(odd, odd_ref[j], even_ref[j])


def own_part(rep, b0, b1, b2):
    def body(rep, b0, b1, b2, out, pack, sems):
        orbitals = b0.shape[0]
        copies = [
            pltpu.make_async_copy(b, pack.at[pl.ds(k * orbitals, orbitals)], sems.at[k])
            for k, b in enumerate((b1, b2))
        ]
        for c in copies:
            c.start()
        products(rep, (b0, b1, b2), [whole(b) for b in (b0, b1, b2)], out)
        for c in copies:
            c.wait()

    pack = jax.ShapeDtypeStruct((2 * b0.shape[0],) + b0.shape[1:], b0.dtype)
    return call(
        body, (acc_shape(b0), pack), [SMEM] + [VMEM] * 3,
        [pltpu.SemaphoreType.DMA((2,))], (VMEM, ANY),
    )(rep, b0, b1, b2)


def next_part(orb, rep, b0, b1, b2, n0, n1x, n2d, n12c):
    def body(orb, rep, b0, b1, b2, n0, n1x, n2d, n12c, out):
        orbitals = b0.shape[0]
        lft = either(orb, n1x, n12c)
        rgt = either(orb, n2d, n12c.at[orbitals:])
        products(rep, (b0, b1, b2), [whole(n0), lft, rgt], out)

    return call(body, acc_shape(b0), [SMEM] * 2 + [VMEM] * 7)(
        orb, rep, b0, b1, b2, n0, n1x, n2d, n12c
    )


def pair_slot(orb, orbs, p, orbitals):
    base = orb[0] * orbitals
    return orbs[0, p] - base, orbs[1, p] - base


def partial_update(orb, rep, orbs, own_acc, next_acc, pre, wgt, b3):
    def body(orb, rep, orbs, own_acc, next_acc, pre, wgt, b3, out, acc):
        orbitals, _, rows, _ = own_acc.shape
        lhs = left_of(rep, (b3,), rows)
        for j in range(orbitals):
            both = dot_t(lhs, b3[j])
            for i in range(orbitals):
                acc[i, j] = own_acc[i, j] + both[i * rows:(i + 1) * rows]

        def pair(p, carry):
            i, j = pair_slot(orb, orbs, p, orbitals)

            @pl.when(j < orbitals)
            def _():
                out[p] = pre[p] - wgt[p] * acc[i, j]

            @pl.when(j >= orbitals)
            def _():
                out[p] = pre[p] - wgt[p] * next_acc[i, j - orbitals]

            return carry

        lax.fori_loop(0, out.shape[0], pair, 0)

    return call(
        body, jax.ShapeDtypeStruct(pre.shape, jnp.float32),
        [SMEM] * 3 + [VMEM] * 5, [pltpu.VMEM(own_acc.shape, own_acc.dtype)],
    )(orb, rep, orbs, own_acc, next_acc, pre, wgt, b3)


def last_update(orb, rep, orbs, part, wgt, left, n3x, n3c):
    def body(orb, rep, orbs, part, wgt, left, n3x, n3c, out, acc, done, sem):
        orbitals = acc.shape[0]
        products(rep, (left,), [either(orb, n3x, n3c)], acc)

        def pair(p, carry):
            i, j = pair_slot(orb, orbs, p, orbitals)

            @pl.when(j >= orbitals)
            def _():
                done[p] = (part[p] - wgt[p] * acc[i, j - orbitals]).astype(done.dtype)

            @pl.when(j < orbitals)
            def _():
                done[p] = part[p].astype(done.dtype)

            pltpu.make_async_copy(done.at[p], out.at[p], sem.at[p]).start()
            return carry

        def wait(p, carry):
            pltpu.make_async_copy(done.at[p], out.at[p], sem.at[p]).wait()
            return carry

        lax.fori_loop(0, done.shape[0], pair, 0)
        lax.fori_loop(0, done.shape[0], wait, 0)

    acc = acc_shape(n3x)
    scratch = [
        pltpu.VMEM(acc.shape, acc.dtype),
        pltpu.VMEM(part.shape, jnp.bfloat16),
        pltpu.SemaphoreType.DMA((part.shape[0],)),
    ]
    return call(
        body, jax.ShapeDtypeStruct(part.shape, jnp.bfloat16),
        [SMEM] * 3 + [VMEM] * 5, scratch, out_specs=ANY,
    )(orb, rep, orbs, part, wgt, left, n3x, n3c)


def device_step(
    blocks, amplitudes, pair_orbitals, coupling, fock_coupling, virtual_energy, occupied_energy
):
    orb = lax.axis_index("orb").astype(jnp.int32).reshape(1)
    rep = lax.axis_index("rep").astype(jnp.int32).reshape(1)
    b0 = blocks
    b1 = along_rep(b0, 1)
    b2 = along_rep(b0, -1)
    n2d = diagonal(b0, -1)
    n0 = along_orb(b0, -1)
    amps_prev = along_orb(amplitudes, 1)
    amps_next = along_orb(amplitudes, -1)
    b3 = along_rep(b1, 1)
    n3x = along_rep_odd(n2d, -1)
    n1x = along_rep_odd(n0, 1)
    own_acc, pack = own_part(rep, b0, b1, b2)
    n12c = swapped(pack)
    n3c = odd_to_even(b3)
    fock = fock_coupling.T.astype(jnp.float32)
    ints = jnp.concatenate([pair_orbitals.T, coupling.T], axis=0)
    energies = jnp.concatenate([occupied_energy[None, :], virtual_energy[None, :]], axis=1)
    pre, wgt = coupled_terms(
        orb, rep, ints, fock, energies, energies,
        amps_prev, amplitudes, amps_next,
    )
    next_acc = next_part(orb, rep, b0, b1, b2, n0, n1x, n2d, n12c)
    part = partial_update(orb, rep, ints, own_acc, next_acc, pre, wgt, b3)
    return last_update(orb, rep, ints, part, wgt, b3, n3x, n3c)


def solution(mesh):
    placed = (
        P("orb", "rep", None),
        P("orb", "rep", None),
        P("orb", None),
        P("orb", None),
        P("orb", None),
        P(),
        P(),
    )
    return jax.shard_map(
        device_step, mesh=mesh, in_specs=placed, out_specs=P("orb", "rep", None), check_vma=False
    )
```

```python
import jax
import jax.numpy as jnp
from jax import lax
from jax.experimental import pallas as pl
from jax.experimental.pallas import tpu as pltpu
from jax.sharding import PartitionSpec as P

damping = 0.7


SMEM = pl.BlockSpec(memory_space=pltpu.SMEM)
VMEM = pl.BlockSpec(memory_space=pltpu.VMEM)
ANY = pl.BlockSpec(memory_space=pl.ANY)


def along_orb(x, distance):
    n = lax.axis_size("orb")
    return lax.ppermute(x, "orb", [(i - distance, i) for i in range(n) if 0 <= i - distance < n])


def along_rep(x, distance):
    n = lax.axis_size("rep")
    return lax.ppermute(x, "rep", [(i, (i + distance) % n) for i in range(n)])


def along_rep_odd(x, distance):
    n, m = lax.axis_size("orb"), lax.axis_size("rep")
    route = [(o * m + i, o * m + (i + distance) % m) for o in range(1, n, 2) for i in range(m)]
    return lax.ppermute(x, ("orb", "rep"), route)


def odd_to_even(x):
    n = lax.axis_size("orb")
    return lax.ppermute(x, "orb", [(o, o - 1) for o in range(1, n, 2)])


def call(body, out_shape, in_specs, scratch=(), out_specs=None, limit=16):
    return pl.pallas_call(
        body,
        out_shape=out_shape,
        in_specs=in_specs,
        out_specs=out_specs or jax.tree.map(lambda _: VMEM, out_shape),
        scratch_shapes=list(scratch),
        compiler_params=pltpu.CompilerParams(vmem_limit_bytes=limit * 2**20),
        cost_estimate=pl.CostEstimate(flops=10**8, bytes_accessed=4 * 2**20, transcendentals=0),
    )


def couple_kernel(ids, orbs, cpl, fock, occ, mine, energy, prev, own, nxt, pre, wgt, amps, sems):
    pair_count, rows = own.shape[:2]
    copies = [
        pltpu.make_async_copy(src, amps.at[pl.ds(k * pair_count, pair_count)], sems.at[k])
        for k, src in enumerate((prev, own, nxt))
    ]
    for c in copies:
        c.start()
    tile = jnp.broadcast_to(mine[...], (rows, rows))

    def denominators(p, carry):
        shift = occ[orbs[0, p]] + occ[orbs[1, p]]
        for c in range(0, energy.shape[1], rows):
            part = slice(c, c + rows)
            wgt[p, :, part] = damping / (tile + (energy[:, part] - shift))
        return carry

    lax.fori_loop(0, pair_count, denominators, 0)
    for c in copies:
        c.wait()
    base = (ids[0] - 1) * pair_count
    step = 32

    def pair(p, carry):
        slots = [cpl[c, p] - base for c in range(cpl.shape[0])]
        scales = [fock[c, p] for c in range(cpl.shape[0])]
        for r in range(0, rows, step):
            part = pl.ds(r, step)
            total = None
            for s, f in zip(slots, scales):
                term = f * amps[s, part, :].astype(jnp.float32)
                total = term if total is None else total + term
            mine = amps[p + pair_count, part, :].astype(jnp.float32)
            pre[p, part, :] = (1.0 - damping) * mine + wgt[p, part, :] * total
        return carry

    lax.fori_loop(0, pair_count, pair, 0)


def coupled_terms(*args):
    own = args[-2]
    shape = jax.ShapeDtypeStruct(own.shape, jnp.float32)
    scratch = (
        pltpu.VMEM((3 * own.shape[0],) + own.shape[1:], own.dtype),
        pltpu.SemaphoreType.DMA((3,)),
    )
    specs = [SMEM] * 5 + [VMEM] * 2 + [ANY] * 3
    return call(couple_kernel, (shape, shape), specs, scratch)(*args)


def dot_t(a, b):
    return lax.dot_general(a, b, (((0,), (0,)), ((), ())), preferred_element_type=jnp.float32)


def left_of(ids, blocks, rows):
    start = pl.multiple_of(ids[1] * rows, rows)
    return jnp.concatenate(
        [
            jnp.concatenate([b[i, :, pl.ds(start, rows)] for i in range(b.shape[0])], axis=1)
            for b in blocks
        ],
        axis=0,
    )


def products(ids, left, right, out, offset=0, base=None):
    orbitals, _, rows, _ = out.shape
    lhs = left_of(ids, left, rows)
    for j in range(left[0].shape[0]):
        both = dot_t(lhs, jnp.concatenate([r(j) for r in right], axis=0))
        for i in range(orbitals):
            part = both[i * rows:(i + 1) * rows]
            out[i, offset + j] = part if base is None else base[i, orbitals + j] + part


def acc_shape(block, columns=1):
    orbitals, _, width = block.shape
    rows = width // lax.axis_size("rep")
    return jax.ShapeDtypeStruct((orbitals, columns * orbitals, rows, width), jnp.float32)


def whole(ref):
    return lambda j: ref[j]


def either(ids, odd_ref, even_ref):
    odd = lax.rem(ids[0], 2) == 1
    return lambda j: jnp.where(odd, odd_ref[j], even_ref[j])


def own_part(ids, b0, b1, b2, n0):
    def body(ids, b0, b1, b2, n0, out):
        products(ids, (b0, b1, b2), [whole(b) for b in (b0, b1, b2)], out)
        products(ids, (b0,), [whole(n0)], out, b0.shape[0])

    return call(body, acc_shape(b0, 2), [SMEM] + [VMEM] * 4)(ids, b0, b1, b2, n0)


def next_part(ids, acc, b1, b2, n1, n2x, n2c):
    def body(ids, acc, b1, b2, n1, n2x, n2c, out):
        products(ids, (b1, b2), [whole(n1), either(ids, n2x, n2c)], out, 0, acc)

    return call(body, acc_shape(b1), [SMEM] + [VMEM] * 6)(ids, acc, b1, b2, n1, n2x, n2c)


def pair_slot(ids, orbs, p, orbitals):
    base = ids[0] * orbitals
    return orbs[0, p] - base, orbs[1, p] - base


def partial_update(ids, orbs, own_acc, next_acc, pre, wgt, b3):
    def body(ids, orbs, own_acc, next_acc, pre, wgt, b3, out, acc):
        orbitals, _, rows, _ = next_acc.shape
        lhs = left_of(ids, (b3,), rows)
        for j in range(orbitals):
            both = dot_t(lhs, b3[j])
            for i in range(orbitals):
                acc[i, j] = own_acc[i, j] + both[i * rows:(i + 1) * rows]

        def pair(p, carry):
            i, j = pair_slot(ids, orbs, p, orbitals)

            @pl.when(j < orbitals)
            def _():
                out[p] = pre[p] - wgt[p] * acc[i, j]

            @pl.when(j >= orbitals)
            def _():
                out[p] = pre[p] - wgt[p] * next_acc[i, j - orbitals]

            return carry

        lax.fori_loop(0, out.shape[0], pair, 0)

    return call(
        body, jax.ShapeDtypeStruct(pre.shape, jnp.float32),
        [SMEM] * 2 + [VMEM] * 5, [pltpu.VMEM(next_acc.shape, next_acc.dtype)],
    )(ids, orbs, own_acc, next_acc, pre, wgt, b3)


def last_update(ids, orbs, part, wgt, left, n3x, n3c):
    def body(ids, orbs, part, wgt, left, n3x, n3c, out, acc, done, sem):
        orbitals = acc.shape[0]
        products(ids, (left,), [either(ids, n3x, n3c)], acc)

        def pair(p, carry):
            i, j = pair_slot(ids, orbs, p, orbitals)

            @pl.when(j >= orbitals)
            def _():
                done[p] = (part[p] - wgt[p] * acc[i, j - orbitals]).astype(done.dtype)

            @pl.when(j < orbitals)
            def _():
                done[p] = part[p].astype(done.dtype)

            pltpu.make_async_copy(done.at[p], out.at[p], sem.at[p]).start()
            return carry

        def wait(p, carry):
            pltpu.make_async_copy(done.at[p], out.at[p], sem.at[p]).wait()
            return carry

        lax.fori_loop(0, done.shape[0], pair, 0)
        lax.fori_loop(0, done.shape[0], wait, 0)

    acc = acc_shape(n3x)
    scratch = [
        pltpu.VMEM(acc.shape, acc.dtype),
        pltpu.VMEM(part.shape, jnp.bfloat16),
        pltpu.SemaphoreType.DMA((part.shape[0],)),
    ]
    return call(
        body, jax.ShapeDtypeStruct(part.shape, jnp.bfloat16),
        [SMEM] * 2 + [VMEM] * 5, scratch, out_specs=ANY,
    )(ids, orbs, part, wgt, left, n3x, n3c)


def device_step(
    blocks, amplitudes, pair_orbitals, coupling, fock_coupling, virtual_energy, occupied_energy
):
    owner = lax.axis_index("orb").astype(jnp.int32)
    replica = lax.axis_index("rep").astype(jnp.int32)
    ids = jnp.stack([owner, replica])
    orbs = pair_orbitals.T
    b0 = blocks
    n0 = along_orb(b0, -1)
    b1 = along_rep(b0, 1)
    b2 = along_rep(b0, -1)
    amps_next = along_orb(amplitudes, -1)
    amps_prev = along_orb(amplitudes, 1)
    n2x = along_rep_odd(n0, -1)
    b3 = along_rep(b1, 1)
    n1 = along_orb(b1, -1)
    n2c = odd_to_even(b2)
    n3x = along_rep_odd(n2x, -1)
    n3c = odd_to_even(b3)
    rows = amplitudes.shape[1]
    row_e = lax.dynamic_slice_in_dim(virtual_energy, replica * rows, rows)[:, None]
    fock = fock_coupling.T.astype(jnp.float32)
    pre, wgt = coupled_terms(
        ids, orbs, coupling.T, fock, occupied_energy, row_e, virtual_energy[None, :],
        amps_prev, amplitudes, amps_next,
    )
    own_acc = own_part(ids, b0, b1, b2, n0)
    next_acc = next_part(ids, own_acc, b1, b2, n1, n2x, n2c)
    part = partial_update(ids, orbs, own_acc, next_acc, pre, wgt, b3)
    return last_update(ids, orbs, part, wgt, b3, n3x, n3c)


def solution(mesh):
    placed = (
        P("orb", "rep", None),
        P("orb", "rep", None),
        P("orb", None),
        P("orb", None),
        P("orb", None),
        P(),
        P(),
    )
    return jax.shard_map(
        device_step, mesh=mesh, in_specs=placed, out_specs=P("orb", "rep", None), check_vma=False
    )
```

```python
import jax
import jax.numpy as jnp
from jax import lax
from jax.experimental import pallas as pl
from jax.experimental.pallas import tpu as pltpu
from jax.sharding import PartitionSpec as P

damping = 0.7


SMEM = pl.BlockSpec(memory_space=pltpu.SMEM)
VMEM = pl.BlockSpec(memory_space=pltpu.VMEM)
ANY = pl.BlockSpec(memory_space=pl.ANY)


def along_orb(x, distance):
    n = lax.axis_size("orb")
    return lax.ppermute(x, "orb", [(i - distance, i) for i in range(n) if 0 <= i - distance < n])


def along_rep(x, distance):
    n = lax.axis_size("rep")
    return lax.ppermute(x, "rep", [(i, (i + distance) % n) for i in range(n)])


def along_rep_odd(x, distance):
    n, m = lax.axis_size("orb"), lax.axis_size("rep")
    route = [(o * m + i, o * m + (i + distance) % m) for o in range(1, n, 2) for i in range(m)]
    return lax.ppermute(x, ("orb", "rep"), route)


def odd_to_even(x):
    n = lax.axis_size("orb")
    return lax.ppermute(x, "orb", [(o, o - 1) for o in range(1, n, 2)])


def call(body, out_shape, in_specs, scratch=(), out_specs=None, limit=16):
    return pl.pallas_call(
        body,
        out_shape=out_shape,
        in_specs=in_specs,
        out_specs=out_specs or jax.tree.map(lambda _: VMEM, out_shape),
        scratch_shapes=list(scratch),
        compiler_params=pltpu.CompilerParams(vmem_limit_bytes=limit * 2**20),
        cost_estimate=pl.CostEstimate(flops=10**8, bytes_accessed=4 * 2**20, transcendentals=0),
    )


def dot_t(a, b):
    return lax.dot_general(a, b, (((0,), (0,)), ((), ())), preferred_element_type=jnp.float32)


def left_of(rep, blocks, rows):
    start = pl.multiple_of(rep[0] * rows, rows)
    return jnp.concatenate(
        [
            jnp.concatenate([b[i, :, pl.ds(start, rows)] for i in range(b.shape[0])], axis=1)
            for b in blocks
        ],
        axis=0,
    )


def products(rep, left, right, out, offset=0, base=None):
    orbitals, _, rows, _ = out.shape
    lhs = left_of(rep, left, rows)
    for j in range(left[0].shape[0]):
        both = dot_t(lhs, jnp.concatenate([r(j) for r in right], axis=0))
        for i in range(orbitals):
            part = both[i * rows:(i + 1) * rows]
            out[i, offset + j] = part if base is None else base[i, offset + j] + part


def acc_shape(block, columns=1):
    orbitals, _, width = block.shape
    rows = width // lax.axis_size("rep")
    return jax.ShapeDtypeStruct((orbitals, columns * orbitals, rows, width), jnp.float32)


def whole(ref):
    return lambda j: ref[j]


def either(orb, odd_ref, even_ref):
    odd = lax.rem(orb[0], 2) == 1
    return lambda j: jnp.where(odd, odd_ref[j], even_ref[j])


def own_part(rep, b0, b1, b2, n0):
    def body(rep, b0, b1, b2, n0, out):
        products(rep, (b0, b1, b2), [whole(b) for b in (b0, b1, b2)], out)
        products(rep, (b0,), [whole(n0)], out, b0.shape[0])

    return call(body, acc_shape(b0, 2), [SMEM] + [VMEM] * 4)(rep, b0, b1, b2, n0)


def pair_slot(orb, ints, p, orbitals):
    base = orb[0] * orbitals
    return ints[0, p] - base, ints[1, p] - base


def middle_kernel(
    orb, rep, ints, fock, occ, energies, base, b1, b2, b3, n1, n2x, n2c, prev, own, nxt,
    part, wgt, acc, amps, sems,
):
    pair_count, rows, width = part.shape
    orbitals = b1.shape[0]
    copies = [
        pltpu.make_async_copy(src, amps.at[pl.ds(k * pair_count, pair_count)], sems.at[k])
        for k, src in enumerate((prev, own, nxt))
    ]
    for c in copies:
        c.start()
    first = energies.shape[1] - width
    mine = energies[:, pl.ds(pl.multiple_of(first + rep[0] * rows, rows), rows)]
    tile = jnp.transpose(jnp.broadcast_to(mine, (rows, rows)))

    def denominators(p, carry):
        shift = occ[0, ints[0, p]] + occ[0, ints[1, p]]
        for c in range(0, width, rows):
            row = energies[:, first + c:first + c + rows]
            wgt[p, :, c:c + rows] = damping / (tile + (row - shift))
        return carry

    lax.fori_loop(0, pair_count, denominators, 0)
    products(rep, (b3,), [whole(b3)], acc, 0, base)
    products(rep, (b1, b2), [whole(n1), either(orb, n2x, n2c)], acc, orbitals, base)
    for c in copies:
        c.wait()
    before = (orb[0] - 1) * pair_count
    step = 32

    def pair(p, carry):
        i, j = pair_slot(orb, ints, p, orbitals)
        slots = [ints[2 + c, p] - before for c in range(fock.shape[0])]
        scales = [fock[c, p] for c in range(fock.shape[0])]
        for r in range(0, rows, step):
            rs = pl.ds(r, step)
            total = -acc[i, j, rs, :]
            for s, f in zip(slots, scales):
                total = total + f * amps[s, rs, :].astype(jnp.float32)
            mine = amps[p + pair_count, rs, :].astype(jnp.float32)
            part[p, rs, :] = (1.0 - damping) * mine + wgt[p, rs, :] * total
        return carry

    lax.fori_loop(0, pair_count, pair, 0)


def middle(*args):
    base, own = args[6], args[-2]
    shape = jax.ShapeDtypeStruct(own.shape, jnp.float32)
    scratch = (
        pltpu.VMEM(base.shape, jnp.float32),
        pltpu.VMEM((3 * own.shape[0],) + own.shape[1:], own.dtype),
        pltpu.SemaphoreType.DMA((3,)),
    )
    specs = [SMEM] * 5 + [VMEM] * 8 + [ANY] * 3
    return call(middle_kernel, (shape, shape), specs, scratch)(*args)


def last_update(orb, rep, ints, part, wgt, b3, n3x, n3c):
    def body(orb, rep, ints, part, wgt, b3, n3x, n3c, out, acc, done, sem):
        orbitals = acc.shape[0]
        products(rep, (b3,), [either(orb, n3x, n3c)], acc)

        def pair(p, carry):
            i, j = pair_slot(orb, ints, p, orbitals)

            @pl.when(j >= orbitals)
            def _():
                done[p] = (part[p] - wgt[p] * acc[i, j - orbitals]).astype(done.dtype)

            @pl.when(j < orbitals)
            def _():
                done[p] = part[p].astype(done.dtype)

            pltpu.make_async_copy(done.at[p], out.at[p], sem.at[p]).start()
            return carry

        def wait(p, carry):
            pltpu.make_async_copy(done.at[p], out.at[p], sem.at[p]).wait()
            return carry

        lax.fori_loop(0, done.shape[0], pair, 0)
        lax.fori_loop(0, done.shape[0], wait, 0)

    acc = acc_shape(b3)
    scratch = [
        pltpu.VMEM(acc.shape, acc.dtype),
        pltpu.VMEM(part.shape, jnp.bfloat16),
        pltpu.SemaphoreType.DMA((part.shape[0],)),
    ]
    return call(
        body, jax.ShapeDtypeStruct(part.shape, jnp.bfloat16),
        [SMEM] * 3 + [VMEM] * 5, scratch, out_specs=ANY,
    )(orb, rep, ints, part, wgt, b3, n3x, n3c)


def device_step(
    blocks, amplitudes, pair_orbitals, coupling, fock_coupling, virtual_energy, occupied_energy
):
    orb = lax.axis_index("orb").astype(jnp.int32).reshape(1)
    rep = lax.axis_index("rep").astype(jnp.int32).reshape(1)
    b0 = blocks
    n0 = along_orb(b0, -1)
    b1 = along_rep(b0, 1)
    b2 = along_rep(b0, -1)
    amps_next = along_orb(amplitudes, -1)
    amps_prev = along_orb(amplitudes, 1)
    n2x = along_rep_odd(n0, -1)
    b3 = along_rep(b1, 1)
    n1 = along_orb(b1, -1)
    n2c = odd_to_even(b2)
    n3x = along_rep_odd(n2x, -1)
    n3c = odd_to_even(b3)
    fock = fock_coupling.T.astype(jnp.float32)
    ints = jnp.concatenate([pair_orbitals.T, coupling.T], axis=0)
    energies = jnp.concatenate([occupied_energy[None, :], virtual_energy[None, :]], axis=1)
    base = own_part(rep, b0, b1, b2, n0)
    part, wgt = middle(
        orb, rep, ints, fock, energies, energies, base, b1, b2, b3, n1, n2x, n2c,
        amps_prev, amplitudes, amps_next,
    )
    return last_update(orb, rep, ints, part, wgt, b3, n3x, n3c)


def solution(mesh):
    placed = (
        P("orb", "rep", None),
        P("orb", "rep", None),
        P("orb", None),
        P("orb", None),
        P("orb", None),
        P(),
        P(),
    )
    return jax.shard_map(
        device_step, mesh=mesh, in_specs=placed, out_specs=P("orb", "rep", None), check_vma=False
    )
```

```python
import jax
import jax.numpy as jnp
from jax import lax
from jax.experimental import pallas as pl
from jax.experimental.pallas import tpu as pltpu
from jax.sharding import PartitionSpec as P

damping = 0.7
ROW = 16


SMEM = pl.BlockSpec(memory_space=pltpu.SMEM)
VMEM = pl.BlockSpec(memory_space=pltpu.VMEM)
ANY = pl.BlockSpec(memory_space=pl.ANY)


def along_orb(x, distance):
    n = lax.axis_size("orb")
    return lax.ppermute(x, "orb", [(i - distance, i) for i in range(n) if 0 <= i - distance < n])


def along_rep(x, distance):
    n = lax.axis_size("rep")
    return lax.ppermute(x, "rep", [(i, (i + distance) % n) for i in range(n)])


def along_rep_odd(x, distance):
    n, m = lax.axis_size("orb"), lax.axis_size("rep")
    route = [(o * m + i, o * m + (i + distance) % m) for o in range(1, n, 2) for i in range(m)]
    return lax.ppermute(x, ("orb", "rep"), route)


def along_rows(x, distance):
    n = lax.axis_size("orb")
    route = [(i - distance, i) for i in range(n) if 0 <= i - distance < n]
    return lax.ppermute(x, "orb", [(s, t) for s, t in route if s // ROW == t // ROW])


def between_rows(x, distance):
    n, m = lax.axis_size("orb"), lax.axis_size("rep")
    route = [(o * m + i, (o - 1) * m + (i + distance) % m) for o in range(ROW, n, ROW) for i in range(m)]
    return lax.ppermute(x, ("orb", "rep"), route)


def odd_to_even(x):
    n = lax.axis_size("orb")
    return lax.ppermute(x, "orb", [(o, o - 1) for o in range(1, n, 2)])


def call(body, out_shape, in_specs, scratch=(), out_specs=None, limit=16):
    return pl.pallas_call(
        body,
        out_shape=out_shape,
        in_specs=in_specs,
        out_specs=out_specs or jax.tree.map(lambda _: VMEM, out_shape),
        scratch_shapes=list(scratch),
        compiler_params=pltpu.CompilerParams(vmem_limit_bytes=limit * 2**20),
        cost_estimate=pl.CostEstimate(flops=10**8, bytes_accessed=4 * 2**20, transcendentals=0),
    )


def couple_kernel(ids, orbs, cpl, fock, occ, mine, energy, prev, own, nxt, pre, wgt, amps, sems):
    pair_count, rows = own.shape[:2]
    copies = [
        pltpu.make_async_copy(src, amps.at[pl.ds(k * pair_count, pair_count)], sems.at[k])
        for k, src in enumerate((prev, own, nxt))
    ]
    for c in copies:
        c.start()
    tile = jnp.broadcast_to(mine[...], (rows, rows))

    def denominators(p, carry):
        shift = occ[orbs[0, p]] + occ[orbs[1, p]]
        for c in range(0, energy.shape[1], rows):
            part = slice(c, c + rows)
            wgt[p, :, part] = damping / (tile + (energy[:, part] - shift))
        return carry

    lax.fori_loop(0, pair_count, denominators, 0)
    for c in copies:
        c.wait()
    base = (ids[0] - 1) * pair_count
    step = 32

    def pair(p, carry):
        slots = [cpl[c, p] - base for c in range(cpl.shape[0])]
        scales = [fock[c, p] for c in range(cpl.shape[0])]
        for r in range(0, rows, step):
            part = pl.ds(r, step)
            total = None
            for s, f in zip(slots, scales):
                term = f * amps[s, part, :].astype(jnp.float32)
                total = term if total is None else total + term
            mine = amps[p + pair_count, part, :].astype(jnp.float32)
            pre[p, part, :] = (1.0 - damping) * mine + wgt[p, part, :] * total
        return carry

    lax.fori_loop(0, pair_count, pair, 0)


def coupled_terms(*args):
    own = args[-2]
    shape = jax.ShapeDtypeStruct(own.shape, jnp.float32)
    scratch = (
        pltpu.VMEM((3 * own.shape[0],) + own.shape[1:], own.dtype),
        pltpu.SemaphoreType.DMA((3,)),
    )
    specs = [SMEM] * 5 + [VMEM] * 2 + [ANY] * 3
    return call(couple_kernel, (shape, shape), specs, scratch)(*args)


def dot_t(a, b):
    return lax.dot_general(a, b, (((0,), (0,)), ((), ())), preferred_element_type=jnp.float32)


def left_of(ids, blocks, rows):
    start = pl.multiple_of(ids[1] * rows, rows)
    return jnp.concatenate(
        [
            jnp.concatenate([b[i, :, pl.ds(start, rows)] for i in range(b.shape[0])], axis=1)
            for b in blocks
        ],
        axis=0,
    )


def products(ids, left, right, out):
    orbitals, _, rows, _ = out.shape
    lhs = left_of(ids, left, rows)
    for j in range(orbitals):
        both = dot_t(lhs, jnp.concatenate([r(j) for r in right], axis=0))
        for i in range(orbitals):
            out[i, j] = both[i * rows:(i + 1) * rows]


def acc_shape(block):
    orbitals, _, width = block.shape
    return jax.ShapeDtypeStruct(
        (orbitals, orbitals, width // lax.axis_size("rep"), width), jnp.float32
    )


def whole(ref):
    return lambda j: ref[j]


def either(ids, odd_ref, even_ref):
    odd = lax.rem(ids[0], 2) == 1
    return lambda j: jnp.where(odd, odd_ref[j], even_ref[j])


def own_part(ids, b0, b1, b2):
    def body(ids, b0, b1, b2, out):
        products(ids, (b0, b1, b2), [whole(b) for b in (b0, b1, b2)], out)

    return call(body, acc_shape(b0), [SMEM] + [VMEM] * 3)(ids, b0, b1, b2)


def next_part(ids, b0, b1, b2, n0, n1, n1e, n2x, n2c):
    def body(ids, b0, b1, b2, n0, n1, n1e, n2x, n2c, out):
        last = lax.rem(ids[0], ROW) == ROW - 1
        lft = lambda j: jnp.where(last, n1e[j], n1[j])
        products(ids, (b0, b1, b2), [whole(n0), lft, either(ids, n2x, n2c)], out)

    return call(body, acc_shape(b0), [SMEM] + [VMEM] * 8)(ids, b0, b1, b2, n0, n1, n1e, n2x, n2c)


def pair_slot(ids, orbs, p, orbitals):
    base = ids[0] * orbitals
    return orbs[0, p] - base, orbs[1, p] - base


def partial_update(ids, orbs, own_acc, next_acc, pre, wgt, b3):
    def body(ids, orbs, own_acc, next_acc, pre, wgt, b3, out, acc):
        orbitals, _, rows, _ = own_acc.shape
        lhs = left_of(ids, (b3,), rows)
        for j in range(orbitals):
            both = dot_t(lhs, b3[j])
            for i in range(orbitals):
                acc[i, j] = own_acc[i, j] + both[i * rows:(i + 1) * rows]

        def pair(p, carry):
            i, j = pair_slot(ids, orbs, p, orbitals)

            @pl.when(j < orbitals)
            def _():
                out[p] = pre[p] - wgt[p] * acc[i, j]

            @pl.when(j >= orbitals)
            def _():
                out[p] = pre[p] - wgt[p] * next_acc[i, j - orbitals]

            return carry

        lax.fori_loop(0, out.shape[0], pair, 0)

    return call(
        body, jax.ShapeDtypeStruct(pre.shape, jnp.float32),
        [SMEM] * 2 + [VMEM] * 5, [pltpu.VMEM(own_acc.shape, own_acc.dtype)],
    )(ids, orbs, own_acc, next_acc, pre, wgt, b3)


def last_update(ids, orbs, part, wgt, left, n3x, n3c):
    def body(ids, orbs, part, wgt, left, n3x, n3c, out, acc, done, sem):
        orbitals = acc.shape[0]
        products(ids, (left,), [either(ids, n3x, n3c)], acc)

        def pair(p, carry):
            i, j = pair_slot(ids, orbs, p, orbitals)

            @pl.when(j >= orbitals)
            def _():
                done[p] = (part[p] - wgt[p] * acc[i, j - orbitals]).astype(done.dtype)

            @pl.when(j < orbitals)
            def _():
                done[p] = part[p].astype(done.dtype)

            pltpu.make_async_copy(done.at[p], out.at[p], sem.at[p]).start()
            return carry

        def wait(p, carry):
            pltpu.make_async_copy(done.at[p], out.at[p], sem.at[p]).wait()
            return carry

        lax.fori_loop(0, done.shape[0], pair, 0)
        lax.fori_loop(0, done.shape[0], wait, 0)

    acc = acc_shape(n3x)
    scratch = [
        pltpu.VMEM(acc.shape, acc.dtype),
        pltpu.VMEM(part.shape, jnp.bfloat16),
        pltpu.SemaphoreType.DMA((part.shape[0],)),
    ]
    return call(
        body, jax.ShapeDtypeStruct(part.shape, jnp.bfloat16),
        [SMEM] * 2 + [VMEM] * 5, scratch, out_specs=ANY,
    )(ids, orbs, part, wgt, left, n3x, n3c)


def device_step(
    blocks, amplitudes, pair_orbitals, coupling, fock_coupling, virtual_energy, occupied_energy
):
    owner = lax.axis_index("orb").astype(jnp.int32)
    replica = lax.axis_index("rep").astype(jnp.int32)
    ids = jnp.stack([owner, replica])
    orbs = pair_orbitals.T
    b0 = blocks
    n0 = along_orb(b0, -1)
    b1 = along_rep(b0, 1)
    b2 = along_rep(b0, -1)
    amps_next = along_orb(amplitudes, -1)
    amps_prev = along_orb(amplitudes, 1)
    n2x = along_rep_odd(n0, -1)
    b3 = along_rep(b1, 1)
    n1 = along_rows(b1, -1)
    n1e = between_rows(b0, 1)
    n2c = odd_to_even(b2)
    n3x = along_rep_odd(n2x, -1)
    n3c = odd_to_even(b3)
    rows = amplitudes.shape[1]
    row_e = lax.dynamic_slice_in_dim(virtual_energy, replica * rows, rows)[:, None]
    fock = fock_coupling.T.astype(jnp.float32)
    pre, wgt = coupled_terms(
        ids, orbs, coupling.T, fock, occupied_energy, row_e, virtual_energy[None, :],
        amps_prev, amplitudes, amps_next,
    )
    own_acc = own_part(ids, b0, b1, b2)
    next_acc = next_part(ids, b0, b1, b2, n0, n1, n1e, n2x, n2c)
    part = partial_update(ids, orbs, own_acc, next_acc, pre, wgt, b3)
    return last_update(ids, orbs, part, wgt, b3, n3x, n3c)


def solution(mesh):
    placed = (
        P("orb", "rep", None),
        P("orb", "rep", None),
        P("orb", None),
        P("orb", None),
        P("orb", None),
        P(),
        P(),
    )
    return jax.shard_map(
        device_step, mesh=mesh, in_specs=placed, out_specs=P("orb", "rep", None), check_vma=False
    )
```

```python
import jax
import jax.numpy as jnp
from jax import lax
from jax.experimental import pallas as pl
from jax.experimental.pallas import tpu as pltpu
from jax.sharding import PartitionSpec as P

damping = 0.7


SMEM = pl.BlockSpec(memory_space=pltpu.SMEM)
VMEM = pl.BlockSpec(memory_space=pltpu.VMEM)
ANY = pl.BlockSpec(memory_space=pl.ANY)


def along_orb(x, distance):
    n = lax.axis_size("orb")
    return lax.ppermute(x, "orb", [(i - distance, i) for i in range(n) if 0 <= i - distance < n])


def along_rep(x, distance):
    n = lax.axis_size("rep")
    return lax.ppermute(x, "rep", [(i, (i + distance) % n) for i in range(n)])


def along_rep_odd(x, distance):
    n, m = lax.axis_size("orb"), lax.axis_size("rep")
    route = [(o * m + i, o * m + (i + distance) % m) for o in range(1, n, 2) for i in range(m)]
    return lax.ppermute(x, ("orb", "rep"), route)


def odd_to_even(x):
    n = lax.axis_size("orb")
    return lax.ppermute(x, "orb", [(o, o - 1) for o in range(1, n, 2)])


def call(body, out_shape, in_specs, scratch):
    return pl.pallas_call(
        body,
        out_shape=out_shape,
        in_specs=in_specs,
        out_specs=jax.tree.map(lambda _: ANY, out_shape),
        scratch_shapes=scratch,
        compiler_params=pltpu.CompilerParams(vmem_limit_bytes=66 * 10**6),
        cost_estimate=pl.CostEstimate(flops=10**9, bytes_accessed=8 * 2**20, transcendentals=0),
    )


def dot_t(a, b):
    return lax.dot_general(a, b, (((0,), (0,)), ((), ())), preferred_element_type=jnp.float32)


def left_of(rep, blocks, rows):
    start = pl.multiple_of(rep[0] * rows, rows)
    return jnp.concatenate(
        [
            jnp.concatenate([b[i, :, pl.ds(start, rows)] for i in range(b.shape[0])], axis=1)
            for b in blocks
        ],
        axis=0,
    )


def products(lhs, right, out, offset=0):
    orbitals, _, rows, _ = out.shape
    for j in range(right[0].shape[0]):
        both = dot_t(lhs, jnp.concatenate([r[j] for r in right], axis=0))
        for i in range(orbitals):
            out[i, offset + j] = both[i * rows:(i + 1) * rows]


def pair_slot(orb, orbs, p, orbitals):
    base = orb[0] * orbitals
    return orbs[0, p] - base, orbs[1, p] - base


def on_odd(orb, odd_copy, even_copy):
    odd = lax.rem(orb[0], 2) == 1

    @pl.when(odd)
    def _():
        odd_copy.start()

    @pl.when(jnp.logical_not(odd))
    def _():
        even_copy.start()


def middle_kernel(
    orb, rep, fock, orbs_in, cpl_in, occ_in, energy_in, b0, b1, b2, b3, n0, n1, n2x, n2c,
    prev, own, nxt, part_out, wgt_out,
    orbs, cpl, occ, energy, mine, after, amps, acc, part, wgt, sems, part_sems, wgt_sem,
):
    pair_count, rows, width = part.shape
    orbitals, depth, _ = b0.shape
    copy = pltpu.make_async_copy
    tables = [
        copy(orbs_in, orbs, sems.at[0]), copy(cpl_in, cpl, sems.at[1]),
        copy(occ_in, occ, sems.at[2]), copy(energy_in, energy, sems.at[3]),
    ]
    first = [copy(b, mine.at[q], sems.at[4 + q]) for q, b in enumerate((b0, b1, b2, b3))]
    second = [copy(b, after.at[q], sems.at[8 + q]) for q, b in enumerate((n0, n1))]
    third = copy(n2x, after.at[2], sems.at[10])
    fourth = [
        copy(a, amps.at[pl.ds(k * pair_count, pair_count)], sems.at[11 + k])
        for k, a in enumerate((prev, own, nxt))
    ]
    for c in tables + first + second:
        c.start()
    on_odd(orb, third, copy(n2c, after.at[2], sems.at[10]))
    for c in fourth:
        c.start()
    for c in tables:
        c.wait()
    energies = energy[:, pl.ds(pl.multiple_of(rep[0] * rows, rows), rows)]
    tile = jnp.transpose(jnp.broadcast_to(energies, (rows, rows)))

    def denominators(p, carry):
        shift = occ[orbs[0, p]] + occ[orbs[1, p]]
        for c in range(0, width, rows):
            wgt[p, :, c:c + rows] = damping / (tile + (energy[:, c:c + rows] - shift))
        return carry

    lax.fori_loop(0, pair_count, denominators, 0)
    wgt_copy = copy(wgt, wgt_out, wgt_sem)
    wgt_copy.start()
    for c in first:
        c.wait()
    quarters = [mine.at[q] for q in range(4)]
    lhs = left_of(rep, quarters, rows)
    products(lhs, quarters, acc)
    for c in second + [third]:
        c.wait()
    products(lhs[:3 * depth], [after.at[q] for q in range(3)], acc, orbitals)
    for c in fourth:
        c.wait()
    before = (orb[0] - 1) * pair_count
    step = 32

    def pair(p, carry):
        i, j = pair_slot(orb, orbs, p, orbitals)
        slots = [cpl[c, p] - before for c in range(cpl.shape[0])]
        scales = [fock[c, p] for c in range(cpl.shape[0])]
        for r in range(0, rows, step):
            rs = pl.ds(r, step)
            total = -acc[i, j, rs, :]
            for s, f in zip(slots, scales):
                total = total + f * amps[s, rs, :].astype(jnp.float32)
            old = amps[p + pair_count, rs, :].astype(jnp.float32)
            part[p, rs, :] = (1.0 - damping) * old + wgt[p, rs, :] * total
        copy(part.at[p], part_out.at[p], part_sems.at[p]).start()
        return carry

    def wait(p, carry):
        copy(part.at[p], part_out.at[p], part_sems.at[p]).wait()
        return carry

    lax.fori_loop(0, pair_count, pair, 0)
    lax.fori_loop(0, pair_count, wait, 0)
    wgt_copy.wait()


def middle(*args):
    orbs, cpl, occ, energy, block = args[3:8]
    own = args[-2]
    orbitals, _, width = block.shape
    pairs, rows, _ = own.shape
    shape = jax.ShapeDtypeStruct(own.shape, jnp.float32)
    scratch = [
        pltpu.SMEM(orbs.shape, orbs.dtype),
        pltpu.SMEM(cpl.shape, cpl.dtype),
        pltpu.SMEM(occ.shape, occ.dtype),
        pltpu.VMEM(energy.shape, energy.dtype),
        pltpu.VMEM((4,) + block.shape, block.dtype),
        pltpu.VMEM((3,) + block.shape, block.dtype),
        pltpu.VMEM((3 * pairs, rows, width), own.dtype),
        pltpu.VMEM((orbitals, 2 * orbitals, rows, width), jnp.float32),
        pltpu.VMEM(own.shape, jnp.float32),
        pltpu.VMEM(own.shape, jnp.float32),
        pltpu.SemaphoreType.DMA((14,)),
        pltpu.SemaphoreType.DMA((pairs,)),
        pltpu.SemaphoreType.DMA,
    ]
    return call(middle_kernel, (shape, shape), [SMEM] * 3 + [ANY] * 15, scratch)(*args)


def last_kernel(
    orb, rep, orbs_in, part_in, wgt_in, b3, n3x, n3c, out,
    orbs, part, wgt, mine, after, acc, done, sems, in_sems, out_sems,
):
    orbitals, _, rows, _ = acc.shape
    copy = pltpu.make_async_copy
    first = [copy(orbs_in, orbs, sems.at[0]), copy(b3, mine, sems.at[1])]
    second = copy(n3x, after, sems.at[2])
    on_odd(orb, second, copy(n3c, after, sems.at[2]))
    for c in first:
        c.start()

    def load(p, carry):
        copy(part_in.at[p], part.at[p], in_sems.at[0, p]).start()
        copy(wgt_in.at[p], wgt.at[p], in_sems.at[1, p]).start()
        return carry

    lax.fori_loop(0, done.shape[0], load, 0)
    for c in first + [second]:
        c.wait()
    products(left_of(rep, [mine], rows), [after], acc)

    def pair(p, carry):
        i, j = pair_slot(orb, orbs, p, orbitals)
        copy(part_in.at[p], part.at[p], in_sems.at[0, p]).wait()
        copy(wgt_in.at[p], wgt.at[p], in_sems.at[1, p]).wait()

        @pl.when(j >= orbitals)
        def _():
            done[p] = (part[p] - wgt[p] * acc[i, j - orbitals]).astype(done.dtype)

        @pl.when(j < orbitals)
        def _():
            done[p] = part[p].astype(done.dtype)

        copy(done.at[p], out.at[p], out_sems.at[p]).start()
        return carry

    def wait(p, carry):
        copy(done.at[p], out.at[p], out_sems.at[p]).wait()
        return carry

    lax.fori_loop(0, done.shape[0], pair, 0)
    lax.fori_loop(0, done.shape[0], wait, 0)


def last_update(*args):
    orbs, part, _, block = args[2:6]
    orbitals, _, width = block.shape
    pairs, rows, _ = part.shape
    scratch = [
        pltpu.SMEM(orbs.shape, orbs.dtype),
        pltpu.VMEM(part.shape, part.dtype),
        pltpu.VMEM(part.shape, part.dtype),
        pltpu.VMEM(block.shape, block.dtype),
        pltpu.VMEM(block.shape, block.dtype),
        pltpu.VMEM((orbitals, orbitals, rows, width), jnp.float32),
        pltpu.VMEM(part.shape, jnp.bfloat16),
        pltpu.SemaphoreType.DMA((3,)),
        pltpu.SemaphoreType.DMA((2, pairs)),
        pltpu.SemaphoreType.DMA((pairs,)),
    ]
    shape = jax.ShapeDtypeStruct(part.shape, jnp.bfloat16)
    return call(last_kernel, shape, [SMEM] * 2 + [ANY] * 6, scratch)(*args)


def device_step(
    blocks, amplitudes, pair_orbitals, coupling, fock_coupling, virtual_energy, occupied_energy
):
    orb = lax.axis_index("orb").astype(jnp.int32).reshape(1)
    rep = lax.axis_index("rep").astype(jnp.int32).reshape(1)
    orbs = pair_orbitals.T
    b0 = blocks
    n0 = along_orb(b0, -1)
    b1 = along_rep(b0, 1)
    b2 = along_rep(b0, -1)
    amps_next = along_orb(amplitudes, -1)
    amps_prev = along_orb(amplitudes, 1)
    n2x = along_rep_odd(n0, -1)
    b3 = along_rep(b1, 1)
    n1 = along_orb(b1, -1)
    n2c = odd_to_even(b2)
    n3x = along_rep_odd(n2x, -1)
    n3c = odd_to_even(b3)
    fock = fock_coupling.T.astype(jnp.float32)
    part, wgt = middle(
        orb, rep, fock, orbs, coupling.T, occupied_energy, virtual_energy[None, :],
        b0, b1, b2, b3, n0, n1, n2x, n2c, amps_prev, amplitudes, amps_next,
    )
    return last_update(orb, rep, orbs, part, wgt, b3, n3x, n3c)


def solution(mesh):
    placed = (
        P("orb", "rep", None),
        P("orb", "rep", None),
        P("orb", None),
        P("orb", None),
        P("orb", None),
        P(),
        P(),
    )
    return jax.shard_map(
        device_step, mesh=mesh, in_specs=placed, out_specs=P("orb", "rep", None), check_vma=False
    )
```

```python
import jax
import jax.numpy as jnp
from jax import lax
from jax.experimental import pallas as pl
from jax.experimental.pallas import tpu as pltpu
from jax.sharding import PartitionSpec as P

damping = 0.7


SMEM = pl.BlockSpec(memory_space=pltpu.SMEM)
VMEM = pl.BlockSpec(memory_space=pltpu.VMEM)
ANY = pl.BlockSpec(memory_space=pl.ANY)


def along_orb(x, distance):
    n = lax.axis_size("orb")
    return lax.ppermute(x, "orb", [(i - distance, i) for i in range(n) if 0 <= i - distance < n])


def along_rep(x, distance):
    n = lax.axis_size("rep")
    return lax.ppermute(x, "rep", [(i, (i + distance) % n) for i in range(n)])


def along_rep_odd(x, distance):
    n, m = lax.axis_size("orb"), lax.axis_size("rep")
    route = [(o * m + i, o * m + (i + distance) % m) for o in range(1, n, 2) for i in range(m)]
    return lax.ppermute(x, ("orb", "rep"), route)


def odd_to_even(x):
    n = lax.axis_size("orb")
    return lax.ppermute(x, "orb", [(o, o - 1) for o in range(1, n, 2)])


def call(body, out_shape, in_specs, scratch=(), out_specs=None, limit=16):
    return pl.pallas_call(
        body,
        out_shape=out_shape,
        in_specs=in_specs,
        out_specs=out_specs or jax.tree.map(lambda _: VMEM, out_shape),
        scratch_shapes=list(scratch),
        compiler_params=pltpu.CompilerParams(vmem_limit_bytes=limit * 2**20),
        cost_estimate=pl.CostEstimate(flops=10**8, bytes_accessed=4 * 2**20, transcendentals=0),
    )


def dot_t(a, b):
    return lax.dot_general(a, b, (((0,), (0,)), ((), ())), preferred_element_type=jnp.float32)


def left_of(blocks, rows):
    start = pl.multiple_of(lax.axis_index("rep") * rows, rows)
    return jnp.concatenate(
        [
            jnp.concatenate([b[i, :, pl.ds(start, rows)] for i in range(b.shape[0])], axis=1)
            for b in blocks
        ],
        axis=0,
    )


def products(left, right, out, offset=0, base=None):
    orbitals, _, rows, _ = out.shape
    lhs = left_of(left, rows)
    for j in range(left[0].shape[0]):
        both = dot_t(lhs, jnp.concatenate([r(j) for r in right], axis=0))
        for i in range(orbitals):
            part = both[i * rows:(i + 1) * rows]
            out[i, offset + j] = part if base is None else base[i, offset + j] + part


def acc_shape(block, columns=1):
    orbitals, _, width = block.shape
    rows = width // lax.axis_size("rep")
    return jax.ShapeDtypeStruct((orbitals, columns * orbitals, rows, width), jnp.float32)


def whole(ref):
    return lambda j: ref[j]


def either(odd_ref, even_ref):
    odd = lax.rem(lax.axis_index("orb"), 2) == 1
    return lambda j: jnp.where(odd, odd_ref[j], even_ref[j])


def own_part(b0, b1, b2, n0):
    def body(b0, b1, b2, n0, out):
        products((b0, b1, b2), [whole(b) for b in (b0, b1, b2)], out)
        products((b0,), [whole(n0)], out, b0.shape[0])

    return call(body, acc_shape(b0, 2), [VMEM] * 4)(b0, b1, b2, n0)


def pair_slot(ints, p, orbitals):
    base = lax.axis_index("orb") * orbitals
    return ints[0, p] - base, ints[1, p] - base


def middle_kernel(
    ints, fock, occ, energies, base, b1, b2, b3, n1, n2x, n2c, prev, own, nxt,
    part, wgt, acc, amps, sems,
):
    pair_count, rows, width = part.shape
    orbitals = b1.shape[0]
    copies = [
        pltpu.make_async_copy(src, amps.at[pl.ds(k * pair_count, pair_count)], sems.at[k])
        for k, src in enumerate((prev, own, nxt))
    ]
    for c in copies:
        c.start()
    first = energies.shape[1] - width
    mine = energies[:, pl.ds(pl.multiple_of(first + lax.axis_index("rep") * rows, rows), rows)]
    tile = jnp.transpose(jnp.broadcast_to(mine, (rows, rows)))

    def denominators(p, carry):
        shift = occ[0, ints[0, p]] + occ[0, ints[1, p]]
        for c in range(0, width, rows):
            row = energies[:, first + c:first + c + rows]
            wgt[p, :, c:c + rows] = damping / (tile + (row - shift))
        return carry

    lax.fori_loop(0, pair_count, denominators, 0)
    products((b3,), [whole(b3)], acc, 0, base)
    products((b1, b2), [whole(n1), either(n2x, n2c)], acc, orbitals, base)
    for c in copies:
        c.wait()
    before = (lax.axis_index("orb") - 1) * pair_count
    step = 32

    def pair(p, carry):
        i, j = pair_slot(ints, p, orbitals)
        slots = [ints[2 + c, p] - before for c in range(fock.shape[0])]
        scales = [fock[c, p] for c in range(fock.shape[0])]
        for r in range(0, rows, step):
            rs = pl.ds(r, step)
            total = -acc[i, j, rs, :]
            for s, f in zip(slots, scales):
                total = total + f * amps[s, rs, :].astype(jnp.float32)
            mine = amps[p + pair_count, rs, :].astype(jnp.float32)
            part[p, rs, :] = (1.0 - damping) * mine + wgt[p, rs, :] * total
        return carry

    lax.fori_loop(0, pair_count, pair, 0)


def middle(*args):
    base, own = args[4], args[-2]
    shape = jax.ShapeDtypeStruct(own.shape, jnp.float32)
    scratch = (
        pltpu.VMEM(base.shape, jnp.float32),
        pltpu.VMEM((3 * own.shape[0],) + own.shape[1:], own.dtype),
        pltpu.SemaphoreType.DMA((3,)),
    )
    specs = [SMEM] * 3 + [VMEM] * 8 + [ANY] * 3
    return call(middle_kernel, (shape, shape), specs, scratch)(*args)


def last_update(ints, part, wgt, b3, n3x, n3c):
    def body(ints, part, wgt, b3, n3x, n3c, out, acc, done, sem):
        orbitals = acc.shape[0]
        products((b3,), [either(n3x, n3c)], acc)

        def pair(p, carry):
            i, j = pair_slot(ints, p, orbitals)

            @pl.when(j >= orbitals)
            def _():
                done[p] = (part[p] - wgt[p] * acc[i, j - orbitals]).astype(done.dtype)

            @pl.when(j < orbitals)
            def _():
                done[p] = part[p].astype(done.dtype)

            pltpu.make_async_copy(done.at[p], out.at[p], sem.at[p]).start()
            return carry

        def wait(p, carry):
            pltpu.make_async_copy(done.at[p], out.at[p], sem.at[p]).wait()
            return carry

        lax.fori_loop(0, done.shape[0], pair, 0)
        lax.fori_loop(0, done.shape[0], wait, 0)

    acc = acc_shape(b3)
    scratch = [
        pltpu.VMEM(acc.shape, acc.dtype),
        pltpu.VMEM(part.shape, jnp.bfloat16),
        pltpu.SemaphoreType.DMA((part.shape[0],)),
    ]
    return call(
        body, jax.ShapeDtypeStruct(part.shape, jnp.bfloat16),
        [SMEM] + [VMEM] * 5, scratch, out_specs=ANY,
    )(ints, part, wgt, b3, n3x, n3c)


def device_step(
    blocks, amplitudes, pair_orbitals, coupling, fock_coupling, virtual_energy, occupied_energy
):
    b0 = blocks
    n0 = along_orb(b0, -1)
    b1 = along_rep(b0, 1)
    b2 = along_rep(b0, -1)
    amps_next = along_orb(amplitudes, -1)
    amps_prev = along_orb(amplitudes, 1)
    n2x = along_rep_odd(n0, -1)
    b3 = along_rep(b1, 1)
    n1 = along_orb(b1, -1)
    n2c = odd_to_even(b2)
    n3x = along_rep_odd(n2x, -1)
    n3c = odd_to_even(b3)
    fock = fock_coupling.T.astype(jnp.float32)
    ints = jnp.concatenate([pair_orbitals.T, coupling.T], axis=0)
    energies = jnp.concatenate([occupied_energy[None, :], virtual_energy[None, :]], axis=1)
    base = own_part(b0, b1, b2, n0)
    part, wgt = middle(
        ints, fock, energies, energies, base, b1, b2, b3, n1, n2x, n2c,
        amps_prev, amplitudes, amps_next,
    )
    return last_update(ints, part, wgt, b3, n3x, n3c)


def solution(mesh):
    placed = (
        P("orb", "rep", None),
        P("orb", "rep", None),
        P("orb", None),
        P("orb", None),
        P("orb", None),
        P(),
        P(),
    )
    return jax.shard_map(
        device_step, mesh=mesh, in_specs=placed, out_specs=P("orb", "rep", None), check_vma=False
    )
```

```python
import jax
import jax.numpy as jnp
from jax import lax
from jax.experimental import pallas as pl
from jax.experimental.pallas import tpu as pltpu
from jax.sharding import PartitionSpec as P

damping = 0.7


SMEM = pl.BlockSpec(memory_space=pltpu.SMEM)
VMEM = pl.BlockSpec(memory_space=pltpu.VMEM)
ANY = pl.BlockSpec(memory_space=pl.ANY)


def along_orb(x, distance):
    n = lax.axis_size("orb")
    return lax.ppermute(x, "orb", [(i - distance, i) for i in range(n) if 0 <= i - distance < n])


def along_rep(x, distance):
    n = lax.axis_size("rep")
    return lax.ppermute(x, "rep", [(i, (i + distance) % n) for i in range(n)])


def along_rep_odd(x, distance):
    n, m = lax.axis_size("orb"), lax.axis_size("rep")
    route = [(o * m + i, o * m + (i + distance) % m) for o in range(1, n, 2) for i in range(m)]
    return lax.ppermute(x, ("orb", "rep"), route)


def odd_to_even(x):
    n = lax.axis_size("orb")
    return lax.ppermute(x, "orb", [(o, o - 1) for o in range(1, n, 2)])


def call(body, out_shape, in_specs, scratch=(), out_specs=None, limit=16):
    return pl.pallas_call(
        body,
        out_shape=out_shape,
        in_specs=in_specs,
        out_specs=out_specs or jax.tree.map(lambda _: VMEM, out_shape),
        scratch_shapes=list(scratch),
        compiler_params=pltpu.CompilerParams(vmem_limit_bytes=limit * 2**20),
        cost_estimate=pl.CostEstimate(flops=10**8, bytes_accessed=4 * 2**20, transcendentals=0),
    )


def dot_t(a, b):
    return lax.dot_general(a, b, (((0,), (0,)), ((), ())), preferred_element_type=jnp.float32)


def left_of(blocks, rows):
    start = pl.multiple_of(lax.axis_index("rep") * rows, rows)
    return jnp.concatenate(
        [
            jnp.concatenate([b[i, :, pl.ds(start, rows)] for i in range(b.shape[0])], axis=1)
            for b in blocks
        ],
        axis=0,
    )


def products(left, right, out, offset=0, base=None):
    orbitals, _, rows, _ = out.shape
    lhs = left_of(left, rows)
    for j in range(left[0].shape[0]):
        both = dot_t(lhs, jnp.concatenate([r(j) for r in right], axis=0))
        for i in range(orbitals):
            part = both[i * rows:(i + 1) * rows]
            out[i, offset + j] = part if base is None else base[i, offset + j] + part


def acc_shape(block, columns=1):
    orbitals, _, width = block.shape
    rows = width // lax.axis_size("rep")
    return jax.ShapeDtypeStruct((orbitals, columns * orbitals, rows, width), jnp.float32)


def whole(ref):
    return lambda j: ref[j]


def either(odd_ref, even_ref):
    odd = lax.rem(lax.axis_index("orb"), 2) == 1
    return lambda j: jnp.where(odd, odd_ref[j], even_ref[j])


def own_part(b0, b1, b2, n0):
    def body(b0, b1, b2, n0, out):
        products((b0, b1, b2), [whole(b) for b in (b0, b1, b2)], out)
        products((b0,), [whole(n0)], out, b0.shape[0])

    return call(body, acc_shape(b0, 2), [VMEM] * 4)(b0, b1, b2, n0)


def pair_slot(ints, p, orbitals):
    base = lax.axis_index("orb") * orbitals
    return ints[0, p] - base, ints[1, p] - base


def middle_kernel(
    orbs, cpl, fock_in, occ, energies, base, b1, b2, b3, n1, n2x, n2c, prev, own, nxt,
    part, wgt, acc, amps, wide, fock, sems,
):
    pair_count, rows, width = part.shape
    orbitals = b1.shape[0]
    copies = [
        pltpu.make_async_copy(src, amps.at[pl.ds(k * pair_count, pair_count)], sems.at[k])
        for k, src in enumerate((prev, own, nxt))
    ]
    wide[...] = fock_in[...].astype(jnp.float32)
    table = pltpu.make_async_copy(wide, fock, sems.at[3])
    table.start()
    for c in copies:
        c.start()
    first = 0
    mine = energies[:, pl.ds(pl.multiple_of(first + lax.axis_index("rep") * rows, rows), rows)]
    tile = jnp.transpose(jnp.broadcast_to(mine, (rows, rows)))

    def denominators(p, carry):
        shift = occ[orbs[0, p]] + occ[orbs[1, p]]
        for c in range(0, width, rows):
            row = energies[:, first + c:first + c + rows]
            wgt[p, :, c:c + rows] = damping / (tile + (row - shift))
        return carry

    lax.fori_loop(0, pair_count, denominators, 0)
    products((b3,), [whole(b3)], acc, 0, base)
    products((b1, b2), [whole(n1), either(n2x, n2c)], acc, orbitals, base)
    table.wait()
    for c in copies:
        c.wait()
    before = (lax.axis_index("orb") - 1) * pair_count
    step = 32

    def pair(p, carry):
        i, j = pair_slot(orbs, p, orbitals)
        slots = [cpl[c, p] - before for c in range(fock.shape[0])]
        scales = [fock[c, p] for c in range(fock.shape[0])]
        for r in range(0, rows, step):
            rs = pl.ds(r, step)
            total = -acc[i, j, rs, :]
            for s, f in zip(slots, scales):
                total = total + f * amps[s, rs, :].astype(jnp.float32)
            mine = amps[p + pair_count, rs, :].astype(jnp.float32)
            part[p, rs, :] = (1.0 - damping) * mine + wgt[p, rs, :] * total
        return carry

    lax.fori_loop(0, pair_count, pair, 0)


def middle(*args):
    base, own = args[5], args[-2]
    shape = jax.ShapeDtypeStruct(own.shape, jnp.float32)
    scratch = (
        pltpu.VMEM(base.shape, jnp.float32),
        pltpu.VMEM((3 * own.shape[0],) + own.shape[1:], own.dtype),
        pltpu.VMEM(args[2].shape, jnp.float32),
        pltpu.SMEM(args[2].shape, jnp.float32),
        pltpu.SemaphoreType.DMA((4,)),
    )
    specs = [SMEM] * 2 + [VMEM, SMEM] + [VMEM] * 8 + [ANY] * 3
    return call(middle_kernel, (shape, shape), specs, scratch)(*args)


def last_update(ints, part, wgt, b3, n3x, n3c):
    def body(ints, part, wgt, b3, n3x, n3c, out, acc, done, sem):
        orbitals = acc.shape[0]
        products((b3,), [either(n3x, n3c)], acc)

        def pair(p, carry):
            i, j = pair_slot(ints, p, orbitals)

            @pl.when(j >= orbitals)
            def _():
                done[p] = (part[p] - wgt[p] * acc[i, j - orbitals]).astype(done.dtype)

            @pl.when(j < orbitals)
            def _():
                done[p] = part[p].astype(done.dtype)

            pltpu.make_async_copy(done.at[p], out.at[p], sem.at[p]).start()
            return carry

        def wait(p, carry):
            pltpu.make_async_copy(done.at[p], out.at[p], sem.at[p]).wait()
            return carry

        lax.fori_loop(0, done.shape[0], pair, 0)
        lax.fori_loop(0, done.shape[0], wait, 0)

    acc = acc_shape(b3)
    scratch = [
        pltpu.VMEM(acc.shape, acc.dtype),
        pltpu.VMEM(part.shape, jnp.bfloat16),
        pltpu.SemaphoreType.DMA((part.shape[0],)),
    ]
    return call(
        body, jax.ShapeDtypeStruct(part.shape, jnp.bfloat16),
        [SMEM] + [VMEM] * 5, scratch, out_specs=ANY,
    )(ints, part, wgt, b3, n3x, n3c)


def device_step(
    blocks, amplitudes, pair_orbitals, coupling, fock_coupling, virtual_energy, occupied_energy
):
    b0 = blocks
    n0 = along_orb(b0, -1)
    b1 = along_rep(b0, 1)
    b2 = along_rep(b0, -1)
    amps_next = along_orb(amplitudes, -1)
    amps_prev = along_orb(amplitudes, 1)
    n2x = along_rep_odd(n0, -1)
    b3 = along_rep(b1, 1)
    n1 = along_orb(b1, -1)
    n2c = odd_to_even(b2)
    n3x = along_rep_odd(n2x, -1)
    n3c = odd_to_even(b3)
    orbs = pair_orbitals.T
    base = own_part(b0, b1, b2, n0)
    part, wgt = middle(
        orbs, coupling.T, fock_coupling.T, occupied_energy, virtual_energy[None, :], base,
        b1, b2, b3, n1, n2x, n2c, amps_prev, amplitudes, amps_next,
    )
    return last_update(orbs, part, wgt, b3, n3x, n3c)


def solution(mesh):
    placed = (
        P("orb", "rep", None),
        P("orb", "rep", None),
        P("orb", None),
        P("orb", None),
        P("orb", None),
        P(),
        P(),
    )
    return jax.shard_map(
        device_step, mesh=mesh, in_specs=placed, out_specs=P("orb", "rep", None), check_vma=False
    )
```

```python
import jax
import jax.numpy as jnp
from jax import lax
from jax.experimental import pallas as pl
from jax.experimental.pallas import tpu as pltpu
from jax.sharding import PartitionSpec as P

damping = 0.7


SMEM = pl.BlockSpec(memory_space=pltpu.SMEM)
VMEM = pl.BlockSpec(memory_space=pltpu.VMEM)
ANY = pl.BlockSpec(memory_space=pl.ANY)


def along_orb(x, distance):
    n = lax.axis_size("orb")
    return lax.ppermute(x, "orb", [(i - distance, i) for i in range(n) if 0 <= i - distance < n])


def along_rep(x, distance):
    n = lax.axis_size("rep")
    return lax.ppermute(x, "rep", [(i, (i + distance) % n) for i in range(n)])


def along_rep_some(x, distance, parity):
    n, m = lax.axis_size("orb"), lax.axis_size("rep")
    route = [
        (o * m + i, o * m + (i + distance) % m) for o in range(parity, n, 2) for i in range(m)
    ]
    return lax.ppermute(x, ("orb", "rep"), route)


def odd_to_even(x):
    n = lax.axis_size("orb")
    return lax.ppermute(x, "orb", [(o, o - 1) for o in range(1, n, 2)])


def call(body, out_shape, in_specs, scratch=(), out_specs=None, limit=16):
    return pl.pallas_call(
        body,
        out_shape=out_shape,
        in_specs=in_specs,
        out_specs=out_specs or jax.tree.map(lambda _: VMEM, out_shape),
        scratch_shapes=list(scratch),
        compiler_params=pltpu.CompilerParams(vmem_limit_bytes=limit * 2**20),
        cost_estimate=pl.CostEstimate(flops=10**8, bytes_accessed=4 * 2**20, transcendentals=0),
    )


def dot_t(a, b):
    return lax.dot_general(a, b, (((0,), (0,)), ((), ())), preferred_element_type=jnp.float32)


def left_of(blocks, rows, orbitals):
    part = pl.ds(pl.multiple_of(lax.axis_index("rep") * rows, rows), rows)
    return jnp.concatenate(
        [jnp.concatenate([b(i, part) for i in range(orbitals)], axis=1) for b in blocks], axis=0
    )


def products(left, right, out, offset=0, base=None):
    orbitals, _, rows, _ = out.shape
    lhs = left_of(left, rows, orbitals)
    for j in range(orbitals):
        both = dot_t(lhs, jnp.concatenate([r(j) for r in right], axis=0))
        for i in range(orbitals):
            part = both[i * rows:(i + 1) * rows]
            out[i, offset + j] = part if base is None else base[i, offset + j] + part


def acc_shape(block, columns=1):
    orbitals, _, width = block.shape
    rows = width // lax.axis_size("rep")
    return jax.ShapeDtypeStruct((orbitals, columns * orbitals, rows, width), jnp.float32)


def whole(ref):
    return lambda j, part=slice(None): ref[j, :, part]


def either(odd_ref, even_ref):
    odd = lax.rem(lax.axis_index("orb"), 2) == 1
    return lambda j, part=slice(None): jnp.where(odd, odd_ref[j, :, part], even_ref[j, :, part])


def own_part(b0, b1, b2, n0):
    def body(b0, b1, b2, n0, out):
        mine = [whole(b) for b in (b0, b1, b2)]
        products(mine, mine, out)
        products(mine[:1], [whole(n0)], out, b0.shape[0])

    return call(body, acc_shape(b0, 2), [VMEM] * 4)(b0, b1, b2, n0)


def pair_slot(ints, p, orbitals):
    base = lax.axis_index("orb") * orbitals
    return ints[0, p] - base, ints[1, p] - base


def middle_kernel(
    orbs, cpl, fock_in, occ, energies, base, b2, b3e, b3o, n2x, n2c, prev, own, nxt,
    part, wgt, acc, amps, wide, fock, sems,
):
    pair_count, rows, width = part.shape
    orbitals = b2.shape[0]
    copies = [
        pltpu.make_async_copy(src, amps.at[pl.ds(k * pair_count, pair_count)], sems.at[k])
        for k, src in enumerate((prev, own, nxt))
    ]
    wide[...] = fock_in[...].astype(jnp.float32)
    table = pltpu.make_async_copy(wide, fock, sems.at[3])
    table.start()
    for c in copies:
        c.start()
    first = 0
    mine = energies[:, pl.ds(pl.multiple_of(first + lax.axis_index("rep") * rows, rows), rows)]
    tile = jnp.transpose(jnp.broadcast_to(mine, (rows, rows)))

    def denominators(p, carry):
        shift = occ[orbs[0, p]] + occ[orbs[1, p]]
        for c in range(0, width, rows):
            row = energies[:, first + c:first + c + rows]
            wgt[p, :, c:c + rows] = damping / (tile + (row - shift))
        return carry

    lax.fori_loop(0, pair_count, denominators, 0)
    opposite = [either(b3o, b3e)]
    products(opposite, opposite, acc, 0, base)
    products([whole(b2)], [either(n2x, n2c)], acc, orbitals, base)
    table.wait()
    for c in copies:
        c.wait()
    before = (lax.axis_index("orb") - 1) * pair_count
    step = 32

    def pair(p, carry):
        i, j = pair_slot(orbs, p, orbitals)
        slots = [cpl[c, p] - before for c in range(fock.shape[0])]
        scales = [fock[c, p] for c in range(fock.shape[0])]
        for r in range(0, rows, step):
            rs = pl.ds(r, step)
            total = -acc[i, j, rs, :]
            for s, f in zip(slots, scales):
                total = total + f * amps[s, rs, :].astype(jnp.float32)
            mine = amps[p + pair_count, rs, :].astype(jnp.float32)
            part[p, rs, :] = (1.0 - damping) * mine + wgt[p, rs, :] * total
        return carry

    lax.fori_loop(0, pair_count, pair, 0)


def middle(*args):
    base, own = args[5], args[-2]
    shape = jax.ShapeDtypeStruct(own.shape, jnp.float32)
    scratch = (
        pltpu.VMEM(base.shape, jnp.float32),
        pltpu.VMEM((3 * own.shape[0],) + own.shape[1:], own.dtype),
        pltpu.VMEM(args[2].shape, jnp.float32),
        pltpu.SMEM(args[2].shape, jnp.float32),
        pltpu.SemaphoreType.DMA((4,)),
    )
    specs = [SMEM] * 2 + [VMEM, SMEM] + [VMEM] * 7 + [ANY] * 3
    return call(middle_kernel, (shape, shape), specs, scratch)(*args)


def last_update(ints, part, wgt, b1, b3e, b3o, n1, n3x, n3c):
    def body(ints, part, wgt, b1, b3e, b3o, n1, n3x, n3c, out, acc, done, sem):
        orbitals = acc.shape[0]
        products([whole(b1), either(b3o, b3e)], [whole(n1), either(n3x, n3c)], acc)

        def pair(p, carry):
            i, j = pair_slot(ints, p, orbitals)

            @pl.when(j >= orbitals)
            def _():
                done[p] = (part[p] - wgt[p] * acc[i, j - orbitals]).astype(done.dtype)

            @pl.when(j < orbitals)
            def _():
                done[p] = part[p].astype(done.dtype)

            pltpu.make_async_copy(done.at[p], out.at[p], sem.at[p]).start()
            return carry

        def wait(p, carry):
            pltpu.make_async_copy(done.at[p], out.at[p], sem.at[p]).wait()
            return carry

        lax.fori_loop(0, done.shape[0], pair, 0)
        lax.fori_loop(0, done.shape[0], wait, 0)

    acc = acc_shape(b1)
    scratch = [
        pltpu.VMEM(acc.shape, acc.dtype),
        pltpu.VMEM(part.shape, jnp.bfloat16),
        pltpu.SemaphoreType.DMA((part.shape[0],)),
    ]
    return call(
        body, jax.ShapeDtypeStruct(part.shape, jnp.bfloat16),
        [SMEM] + [VMEM] * 8, scratch, out_specs=ANY,
    )(ints, part, wgt, b1, b3e, b3o, n1, n3x, n3c)


def device_step(
    blocks, amplitudes, pair_orbitals, coupling, fock_coupling, virtual_energy, occupied_energy
):
    b0 = blocks
    n0 = along_orb(b0, -1)
    b1 = along_rep(b0, 1)
    b2 = along_rep(b0, -1)
    amps_next = along_orb(amplitudes, -1)
    amps_prev = along_orb(amplitudes, 1)
    n2x = along_rep_some(n0, -1, 1)
    b3e = along_rep_some(b1, 1, 0)
    b3o = along_rep_some(b2, -1, 1)
    n1 = along_orb(b1, -1)
    n2c = odd_to_even(b2)
    n3x = along_rep_some(n2x, -1, 1)
    n3c = odd_to_even(b3o)
    orbs = pair_orbitals.T
    base = own_part(b0, b1, b2, n0)
    part, wgt = middle(
        orbs, coupling.T, fock_coupling.T, occupied_energy, virtual_energy[None, :], base,
        b2, b3e, b3o, n2x, n2c, amps_prev, amplitudes, amps_next,
    )
    return last_update(orbs, part, wgt, b1, b3e, b3o, n1, n3x, n3c)


def solution(mesh):
    placed = (
        P("orb", "rep", None),
        P("orb", "rep", None),
        P("orb", None),
        P("orb", None),
        P("orb", None),
        P(),
        P(),
    )
    return jax.shard_map(
        device_step, mesh=mesh, in_specs=placed, out_specs=P("orb", "rep", None), check_vma=False
    )
```

```python
import jax
import jax.numpy as jnp
from jax import lax
from jax.experimental import pallas as pl
from jax.experimental.pallas import tpu as pltpu
from jax.sharding import PartitionSpec as P

damping = 0.7


SMEM = pl.BlockSpec(memory_space=pltpu.SMEM)
VMEM = pl.BlockSpec(memory_space=pltpu.VMEM)
ANY = pl.BlockSpec(memory_space=pl.ANY)


def along_orb(x, distance):
    n = lax.axis_size("orb")
    return lax.ppermute(x, "orb", [(i - distance, i) for i in range(n) if 0 <= i - distance < n])


def along_rep(x, distance):
    n = lax.axis_size("rep")
    return lax.ppermute(x, "rep", [(i, (i + distance) % n) for i in range(n)])


def along_rep_odd(x, distance):
    n, m = lax.axis_size("orb"), lax.axis_size("rep")
    route = [(o * m + i, o * m + (i + distance) % m) for o in range(1, n, 2) for i in range(m)]
    return lax.ppermute(x, ("orb", "rep"), route)


def odd_to_even(x):
    n = lax.axis_size("orb")
    return lax.ppermute(x, "orb", [(o, o - 1) for o in range(1, n, 2)])


def call(body, out_shape, in_specs, scratch=(), out_specs=None, limit=16):
    return pl.pallas_call(
        body,
        out_shape=out_shape,
        in_specs=in_specs,
        out_specs=out_specs or jax.tree.map(lambda _: VMEM, out_shape),
        scratch_shapes=list(scratch),
        compiler_params=pltpu.CompilerParams(vmem_limit_bytes=limit * 2**20),
        cost_estimate=pl.CostEstimate(flops=10**8, bytes_accessed=4 * 2**20, transcendentals=0),
    )


def dot_t(a, b):
    return lax.dot_general(a, b, (((0,), (0,)), ((), ())), preferred_element_type=jnp.float32)


def left_of(blocks, rows):
    start = pl.multiple_of(lax.axis_index("rep") * rows, rows)
    return jnp.concatenate(
        [
            jnp.concatenate([b[i, :, pl.ds(start, rows)] for i in range(b.shape[0])], axis=1)
            for b in blocks
        ],
        axis=0,
    )


def products(left, right, out, offset=0, base=None):
    orbitals, _, rows, _ = out.shape
    lhs = left_of(left, rows)
    for j in range(left[0].shape[0]):
        both = dot_t(lhs, jnp.concatenate([r(j) for r in right], axis=0))
        for i in range(orbitals):
            part = both[i * rows:(i + 1) * rows]
            out[i, offset + j] = part if base is None else base[i, offset + j] + part


def acc_shape(block, columns=1):
    orbitals, _, width = block.shape
    rows = width // lax.axis_size("rep")
    return jax.ShapeDtypeStruct((orbitals, columns * orbitals, rows, width), jnp.float32)


def whole(ref):
    return lambda j: ref[j]


def either(odd_ref, even_ref):
    odd = lax.rem(lax.axis_index("orb"), 2) == 1
    return lambda j: jnp.where(odd, odd_ref[j], even_ref[j])


def own_part(b0, b1, b2, n0):
    def body(b0, b1, b2, n0, out):
        products((b0, b1, b2), [whole(b) for b in (b0, b1, b2)], out)
        products((b0,), [whole(n0)], out, b0.shape[0])

    return call(body, acc_shape(b0, 2), [VMEM] * 4)(b0, b1, b2, n0)


def pair_slot(ints, p, orbitals):
    base = lax.axis_index("orb") * orbitals
    return ints[0, p] - base, ints[1, p] - base


def middle_kernel(
    orbs, cpl, fock_in, occ, energies, base, b2, b3, n2x, n2c, prev, own, nxt,
    part, wgt, acc, amps, wide, fock, sems,
):
    pair_count, rows, width = part.shape
    orbitals = b2.shape[0]
    copies = [
        pltpu.make_async_copy(src, amps.at[pl.ds(k * pair_count, pair_count)], sems.at[k])
        for k, src in enumerate((prev, own, nxt))
    ]
    wide[...] = fock_in[...].astype(jnp.float32)
    table = pltpu.make_async_copy(wide, fock, sems.at[3])
    table.start()
    for c in copies:
        c.start()
    first = 0
    mine = energies[:, pl.ds(pl.multiple_of(first + lax.axis_index("rep") * rows, rows), rows)]
    tile = jnp.transpose(jnp.broadcast_to(mine, (rows, rows)))

    def denominators(p, carry):
        shift = occ[orbs[0, p]] + occ[orbs[1, p]]
        for c in range(0, width, rows):
            row = energies[:, first + c:first + c + rows]
            wgt[p, :, c:c + rows] = damping / (tile + (row - shift))
        return carry

    lax.fori_loop(0, pair_count, denominators, 0)
    products((b3,), [whole(b3)], acc, 0, base)
    products((b2,), [either(n2x, n2c)], acc, orbitals, base)
    table.wait()
    for c in copies:
        c.wait()
    before = (lax.axis_index("orb") - 1) * pair_count
    step = 32

    def pair(p, carry):
        i, j = pair_slot(orbs, p, orbitals)
        slots = [cpl[c, p] - before for c in range(fock.shape[0])]
        scales = [fock[c, p] for c in range(fock.shape[0])]
        for r in range(0, rows, step):
            rs = pl.ds(r, step)
            total = -acc[i, j, rs, :]
            for s, f in zip(slots, scales):
                total = total + f * amps[s, rs, :].astype(jnp.float32)
            mine = amps[p + pair_count, rs, :].astype(jnp.float32)
            part[p, rs, :] = (1.0 - damping) * mine + wgt[p, rs, :] * total
        return carry

    lax.fori_loop(0, pair_count, pair, 0)


def middle(*args):
    base, own = args[5], args[-2]
    shape = jax.ShapeDtypeStruct(own.shape, jnp.float32)
    scratch = (
        pltpu.VMEM(base.shape, jnp.float32),
        pltpu.VMEM((3 * own.shape[0],) + own.shape[1:], own.dtype),
        pltpu.VMEM(args[2].shape, jnp.float32),
        pltpu.SMEM(args[2].shape, jnp.float32),
        pltpu.SemaphoreType.DMA((4,)),
    )
    specs = [SMEM] * 2 + [VMEM, SMEM] + [VMEM] * 6 + [ANY] * 3
    return call(middle_kernel, (shape, shape), specs, scratch)(*args)


def last_update(ints, part, wgt, b1, b3, n1, n3x, n3c):
    def body(ints, part, wgt, b1, b3, n1, n3x, n3c, out, acc, done, sem):
        orbitals = acc.shape[0]
        write = lambda p: pltpu.make_async_copy(done.at[p], out.at[p], sem.at[p])

        def settled(p, carry):
            _, j = pair_slot(ints, p, orbitals)

            @pl.when(j < orbitals)
            def _():
                done[p] = part[p].astype(done.dtype)
                write(p).start()

            return carry

        lax.fori_loop(0, done.shape[0], settled, 0)
        products((b1, b3), [whole(n1), either(n3x, n3c)], acc)

        def pair(p, carry):
            i, j = pair_slot(ints, p, orbitals)

            @pl.when(j >= orbitals)
            def _():
                done[p] = (part[p] - wgt[p] * acc[i, j - orbitals]).astype(done.dtype)
                write(p).start()

            return carry

        def wait(p, carry):
            pltpu.make_async_copy(done.at[p], out.at[p], sem.at[p]).wait()
            return carry

        lax.fori_loop(0, done.shape[0], pair, 0)
        lax.fori_loop(0, done.shape[0], wait, 0)

    acc = acc_shape(b3)
    scratch = [
        pltpu.VMEM(acc.shape, acc.dtype),
        pltpu.VMEM(part.shape, jnp.bfloat16),
        pltpu.SemaphoreType.DMA((part.shape[0],)),
    ]
    return call(
        body, jax.ShapeDtypeStruct(part.shape, jnp.bfloat16),
        [SMEM] + [VMEM] * 7, scratch, out_specs=ANY,
    )(ints, part, wgt, b1, b3, n1, n3x, n3c)


def device_step(
    blocks, amplitudes, pair_orbitals, coupling, fock_coupling, virtual_energy, occupied_energy
):
    b0 = blocks
    n0 = along_orb(b0, -1)
    b1 = along_rep(b0, 1)
    b2 = along_rep(b0, -1)
    amps_next = along_orb(amplitudes, -1)
    amps_prev = along_orb(amplitudes, 1)
    n2x = along_rep_odd(n0, -1)
    b3 = along_rep(b1, 1)
    n1 = along_orb(b1, -1)
    n2c = odd_to_even(b2)
    n3x = along_rep_odd(n2x, -1)
    n3c = odd_to_even(b3)
    orbs = pair_orbitals.T
    base = own_part(b0, b1, b2, n0)
    part, wgt = middle(
        orbs, coupling.T, fock_coupling.T, occupied_energy, virtual_energy[None, :], base,
        b2, b3, n2x, n2c, amps_prev, amplitudes, amps_next,
    )
    return last_update(orbs, part, wgt, b1, b3, n1, n3x, n3c)


def solution(mesh):
    placed = (
        P("orb", "rep", None),
        P("orb", "rep", None),
        P("orb", None),
        P("orb", None),
        P("orb", None),
        P(),
        P(),
    )
    return jax.shard_map(
        device_step, mesh=mesh, in_specs=placed, out_specs=P("orb", "rep", None), check_vma=False
    )
```

```python
import jax
import jax.numpy as jnp
from jax import lax
from jax.experimental import pallas as pl
from jax.experimental.pallas import tpu as pltpu
from jax.sharding import PartitionSpec as P

damping = 0.7


SMEM = pl.BlockSpec(memory_space=pltpu.SMEM)
VMEM = pl.BlockSpec(memory_space=pltpu.VMEM)
ANY = pl.BlockSpec(memory_space=pl.ANY)


def along_orb(x, distance):
    n = lax.axis_size("orb")
    return lax.ppermute(x, "orb", [(i - distance, i) for i in range(n) if 0 <= i - distance < n])


def along_rep(x, distance):
    n = lax.axis_size("rep")
    return lax.ppermute(x, "rep", [(i, (i + distance) % n) for i in range(n)])


def along_rep_odd(x, distance):
    n, m = lax.axis_size("orb"), lax.axis_size("rep")
    route = [(o * m + i, o * m + (i + distance) % m) for o in range(1, n, 2) for i in range(m)]
    return lax.ppermute(x, ("orb", "rep"), route)


def odd_to_even(x):
    n = lax.axis_size("orb")
    return lax.ppermute(x, "orb", [(o, o - 1) for o in range(1, n, 2)])


def call(body, out_shape, in_specs, scratch=(), out_specs=None, limit=16):
    return pl.pallas_call(
        body,
        out_shape=out_shape,
        in_specs=in_specs,
        out_specs=out_specs or jax.tree.map(lambda _: VMEM, out_shape),
        scratch_shapes=list(scratch),
        compiler_params=pltpu.CompilerParams(vmem_limit_bytes=limit * 2**20),
        cost_estimate=pl.CostEstimate(flops=10**8, bytes_accessed=4 * 2**20, transcendentals=0),
    )


def dot_t(a, b):
    return lax.dot_general(a, b, (((0,), (0,)), ((), ())), preferred_element_type=jnp.float32)


def left_of(blocks, rows):
    start = pl.multiple_of(lax.axis_index("rep") * rows, rows)
    return jnp.concatenate(
        [
            jnp.concatenate([b[i, :, pl.ds(start, rows)] for i in range(b.shape[0])], axis=1)
            for b in blocks
        ],
        axis=0,
    )


def products(left, right, out, offset=0, base=None):
    orbitals, _, rows, _ = out.shape
    lhs = left_of(left, rows)
    for j in range(left[0].shape[0]):
        both = dot_t(lhs, jnp.concatenate([r(j) for r in right], axis=0))
        for i in range(orbitals):
            part = both[i * rows:(i + 1) * rows]
            out[i, offset + j] = part if base is None else base[i, offset + j] + part


def acc_shape(block, columns=1):
    orbitals, _, width = block.shape
    rows = width // lax.axis_size("rep")
    return jax.ShapeDtypeStruct((orbitals, columns * orbitals, rows, width), jnp.float32)


def whole(ref):
    return lambda j: ref[j]


def either(odd_ref, even_ref):
    odd = lax.rem(lax.axis_index("orb"), 2) == 1
    return lambda j: jnp.where(odd, odd_ref[j], even_ref[j])


def own_part(b0, b1, b2, n0):
    def body(b0, b1, b2, n0, out):
        products((b0, b1, b2), [whole(b) for b in (b0, b1, b2)], out)
        products((b0,), [whole(n0)], out, b0.shape[0])

    return call(body, acc_shape(b0, 2), [VMEM] * 4)(b0, b1, b2, n0)


def pair_slot(ints, p, orbitals):
    base = lax.axis_index("orb") * orbitals
    return ints[0, p] - base, ints[1, p] - base


def middle_kernel(
    orbs, cpl, fock_in, occ, energies, base, b2, b3, n2x, n2c, prev, own, nxt,
    part, wgt, acc, amps, wide, fock, sems,
):
    pair_count, rows, width = part.shape
    orbitals = b2.shape[0]
    copies = [
        pltpu.make_async_copy(src, amps.at[pl.ds(k * pair_count, pair_count)], sems.at[k])
        for k, src in enumerate((prev, own, nxt))
    ]
    wide[...] = fock_in[...].astype(jnp.float32)
    table = pltpu.make_async_copy(wide, fock, sems.at[3])
    table.start()
    for c in copies:
        c.start()
    first = 0
    mine = energies[:, pl.ds(pl.multiple_of(first + lax.axis_index("rep") * rows, rows), rows)]
    tile = jnp.transpose(jnp.broadcast_to(mine, (rows, rows)))

    def denominators(p, carry):
        shift = occ[orbs[0, p]] + occ[orbs[1, p]]
        for c in range(0, width, rows):
            row = energies[:, first + c:first + c + rows]
            wgt[p, :, c:c + rows] = damping / (tile + (row - shift))
        return carry

    lax.fori_loop(0, pair_count, denominators, 0)
    products((b3,), [whole(b3)], acc, 0, base)
    products((b2,), [either(n2x, n2c)], acc, orbitals, base)
    table.wait()
    for c in copies:
        c.wait()
    before = (lax.axis_index("orb") - 1) * pair_count
    step = 32

    def pair(p, carry):
        i, j = pair_slot(orbs, p, orbitals)
        slots = [cpl[c, p] - before for c in range(fock.shape[0])]
        scales = [fock[c, p] for c in range(fock.shape[0])]
        for r in range(0, rows, step):
            rs = pl.ds(r, step)
            total = -acc[i, j, rs, :]
            for s, f in zip(slots, scales):
                total = total + f * amps[s, rs, :].astype(jnp.float32)
            mine = amps[p + pair_count, rs, :].astype(jnp.float32)
            part[p, rs, :] = (1.0 - damping) * mine + wgt[p, rs, :] * total
        return carry

    lax.fori_loop(0, pair_count, pair, 0)


def middle(*args):
    base, own = args[5], args[-2]
    shape = jax.ShapeDtypeStruct(own.shape, jnp.float32)
    scratch = (
        pltpu.VMEM(base.shape, jnp.float32),
        pltpu.VMEM((3 * own.shape[0],) + own.shape[1:], own.dtype),
        pltpu.VMEM(args[2].shape, jnp.float32),
        pltpu.SMEM(args[2].shape, jnp.float32),
        pltpu.SemaphoreType.DMA((4,)),
    )
    specs = [SMEM] * 2 + [VMEM, SMEM] + [VMEM] * 6 + [ANY] * 3
    return call(middle_kernel, (shape, shape), specs, scratch)(*args)


def last_update(ints, part, wgt, b1, b3, n1, n3x, n3c):
    def body(ints, part, wgt, b1, b3, n1, n3x, n3c, out, acc, done, sem):
        orbitals = acc.shape[0]
        products((b1, b3), [whole(n1), either(n3x, n3c)], acc)

        def pair(p, carry):
            i, j = pair_slot(ints, p, orbitals)

            @pl.when(j >= orbitals)
            def _():
                done[p] = (part[p] - wgt[p] * acc[i, j - orbitals]).astype(done.dtype)

            @pl.when(j < orbitals)
            def _():
                done[p] = part[p].astype(done.dtype)

            pltpu.make_async_copy(done.at[p], out.at[p], sem.at[p]).start()
            return carry

        def wait(p, carry):
            pltpu.make_async_copy(done.at[p], out.at[p], sem.at[p]).wait()
            return carry

        lax.fori_loop(0, done.shape[0], pair, 0, unroll=4)
        lax.fori_loop(0, done.shape[0], wait, 0)

    acc = acc_shape(b3)
    scratch = [
        pltpu.VMEM(acc.shape, acc.dtype),
        pltpu.VMEM(part.shape, jnp.bfloat16),
        pltpu.SemaphoreType.DMA((part.shape[0],)),
    ]
    return call(
        body, jax.ShapeDtypeStruct(part.shape, jnp.bfloat16),
        [SMEM] + [VMEM] * 7, scratch, out_specs=ANY,
    )(ints, part, wgt, b1, b3, n1, n3x, n3c)


def device_step(
    blocks, amplitudes, pair_orbitals, coupling, fock_coupling, virtual_energy, occupied_energy
):
    b0 = blocks
    n0 = along_orb(b0, -1)
    b1 = along_rep(b0, 1)
    b2 = along_rep(b0, -1)
    amps_next = along_orb(amplitudes, -1)
    amps_prev = along_orb(amplitudes, 1)
    n2x = along_rep_odd(n0, -1)
    b3 = along_rep(b1, 1)
    n1 = along_orb(b1, -1)
    n2c = odd_to_even(b2)
    n3x = along_rep_odd(n2x, -1)
    n3c = odd_to_even(b3)
    orbs = pair_orbitals.T
    base = own_part(b0, b1, b2, n0)
    part, wgt = middle(
        orbs, coupling.T, fock_coupling.T, occupied_energy, virtual_energy[None, :], base,
        b2, b3, n2x, n2c, amps_prev, amplitudes, amps_next,
    )
    return last_update(orbs, part, wgt, b1, b3, n1, n3x, n3c)


def solution(mesh):
    placed = (
        P("orb", "rep", None),
        P("orb", "rep", None),
        P("orb", None),
        P("orb", None),
        P("orb", None),
        P(),
        P(),
    )
    return jax.shard_map(
        device_step, mesh=mesh, in_specs=placed, out_specs=P("orb", "rep", None), check_vma=False
    )
```
